512 devices in a mesh: pages: 128 (over x, z, core), queries: 4 (over y).
Axes of the slice: x: 4, y: 4, z: 16, core: 2. Of those that a mesh axis runs over, the one named last changes fastest.
Arguments:
- query_tokens: bfloat16 [128, 32, 128], P('pages'), may hold values from -1 to 1
- page_patches: bfloat16 [256, 1536, 128], P('pages', 'queries'), may hold values from -1 to 1, as said below
- patch_counts: int32 [256], P('pages'), may hold values from 512 to 1536, as said below
- positive_page: int32 [128], replicated, may hold values from 0 to 255
Outputs:
- query_loss: float32 [128], replicated
- query_grad: float32 [128, 32, 128], P('pages', 'queries')
- page_grad: float32 [256, 1536, 128], P('pages', 'queries')
The draws below stay inside these ranges and needn't reach their ends.
Inputs may be any that keep to these rules, and one draw needn't show every extreme that they name: `patch_counts`: each page's number of valid patches; some page has exactly 1536. `page_patches`: slots at or past a page's count hold arbitrary values.
All inputs are finite; a program needn't handle non-finite values.
Results may differ from the reference program's by a relative error of at most 0.0028.
Values may be sent and summed in bfloat16 or wider, within the bound.
A program may use at most 64 MiB of HBM per device.

```python
import jax
import jax.numpy as jnp
from jax import lax

E = 128
QT = 32
MAXP = 1536
MINP = 512
NQ = 128
NPG = 256


def layout(key):
    base_key = jax.random.fold_in(key, 7001)
    counts_all = jax.random.randint(jax.random.fold_in(base_key, 1), (NPG,), MINP, MAXP + 1)
    page_order = jax.random.permutation(jax.random.fold_in(base_key, 2), NPG)
    first = page_order[:4]
    second = page_order[4:8]
    counts_all = counts_all.at[first[0]].set(MAXP)
    counts_all = counts_all.at[second].set(counts_all[first])
    return counts_all


def page_scale():
    position = jnp.arange(NPG, dtype=jnp.float32) / NPG
    return (0.25 * jnp.exp2(position))[:, None, None]


def draw_patch_counts(key, part):
    counts_all = layout(key)
    return counts_all.astype(jnp.int32)


def draw_query_tokens(key, part):
    own_key = jax.random.fold_in(key, 11)
    values = jnp.clip(jax.random.normal(own_key, (NQ, QT, E)), -3.0, 3.0) * 0.25 / jnp.sqrt(E * 1.0)
    return values.astype(jnp.bfloat16)


def draw_page_patches(key, part):
    own_key = jax.random.fold_in(key, 13)
    values = jnp.clip(jax.random.normal(own_key, (NPG, MAXP, E)), -3.0, 3.0) * page_scale() / jnp.sqrt(E * 1.0)
    return values.astype(jnp.bfloat16)


def place_ends(entries, rng, smallest, largest):
    place = [jax.random.randint(jax.random.fold_in(rng, axis), (), 0, length) for axis, length in enumerate(entries.shape)]
    widest = entries.shape.index(max(entries.shape))
    next_to = place[:widest] + [(place[widest] + 1) % entries.shape[widest]] + place[widest + 1:]
    return entries.at[tuple(place)].set(smallest).at[tuple(next_to)].set(largest)


def setup_inputs(seed: int = 0) -> dict:
    keys = jax.random.split(jax.random.key(seed), 5)
    return {
        "query_tokens": draw_query_tokens(jax.random.fold_in(keys[4], 71), 0),
        "page_patches": draw_page_patches(jax.random.fold_in(keys[4], 71), 0),
        "patch_counts": draw_patch_counts(jax.random.fold_in(keys[4], 71), 0),
        "positive_page": place_ends(jax.random.randint(keys[3], (NQ,), 0, NPG), jax.random.fold_in(keys[3], 1), 0, NPG - 1).astype(jnp.int32),
    }


smooth_tau = 0.05
page_temp = 0.02


def page_similar(token_rows, page_rows, count_now):
    similar = jnp.dot(token_rows, page_rows.T, preferred_element_type=jnp.float32)
    valid_mask = jnp.arange(page_rows.shape[0], dtype=jnp.int32) < count_now
    masked = jnp.where(valid_mask[None, :], similar, -1e30)
    return masked, valid_mask


def reference(query_tokens, page_patches, patch_counts, positive_page):
    query_count, query_len, embed_width = query_tokens.shape
    page_total = page_patches.shape[0]
    token_rows = query_tokens.reshape(query_count * query_len, embed_width)

    def forward(item):
        page_rows, count_now = item
        masked, valid_mask = page_similar(token_rows, page_rows, count_now)
        highest = jnp.max(masked, axis=1)
        terms = jnp.where(valid_mask[None, :], jnp.exp((masked - highest[:, None]) / smooth_tau), 0.0)
        return highest + smooth_tau * jnp.log(jnp.sum(terms, axis=1))

    patch_lse = lax.map(forward, (page_patches, patch_counts))
    smooth = patch_lse - smooth_tau * jnp.log(patch_counts.astype(jnp.float32))[:, None]
    logits = smooth.reshape(page_total, query_count, query_len).sum(axis=2).T / page_temp
    highest = jnp.max(logits, axis=1)
    page_sum = jnp.sum(jnp.exp(logits - highest[:, None]), axis=1)
    is_positive = jnp.arange(page_total, dtype=jnp.int32)[None, :] == positive_page[:, None]
    query_loss = highest + jnp.log(page_sum) - jnp.sum(jnp.where(is_positive, logits, 0.0), axis=1)
    weights = (jnp.exp(logits - highest[:, None]) / page_sum[:, None] - is_positive.astype(jnp.float32)) / page_temp
    row_weights = jnp.broadcast_to(weights.T[:, :, None], (page_total, query_count, query_len)).reshape(page_total, query_count * query_len)

    def backward(grad_rows, item):
        page_rows, count_now, page_lse, page_weight = item
        masked, valid_mask = page_similar(token_rows, page_rows, count_now)
        prob_tile = jnp.where(valid_mask[None, :], jnp.exp((masked - page_lse[:, None]) / smooth_tau), 0.0)
        coef_tile = (page_weight[:, None] * prob_tile).astype(jnp.bfloat16)
        grad_rows = grad_rows + jnp.dot(coef_tile, page_rows, preferred_element_type=jnp.float32)
        page_grad = jnp.dot(coef_tile.T, token_rows, preferred_element_type=jnp.float32)
        return grad_rows, page_grad

    start_grad = jnp.zeros((query_count * query_len, embed_width), jnp.float32)
    grad_rows, page_grad = lax.scan(backward, start_grad, (page_patches, patch_counts, patch_lse, row_weights))
    return query_loss, grad_rows.reshape(query_count, query_len, embed_width), page_grad
```

```python
import functools

import jax
import jax.numpy as jnp
from jax import lax
from jax.experimental import pallas as pl
from jax.experimental.pallas import tpu as pltpu
from jax.sharding import PartitionSpec as P

smooth_tau = 0.05
page_temp = 0.02
neg_large = -1e30
chips_z = 16
lane_chunk = 256
MESH = pl.DeviceIdType.MESH
f32, bf16 = jnp.float32, jnp.bfloat16


def ring_offsets(count):
    near = sorted(range(count), key=lambda d: (min(d, count - d), d))
    return near


def onehot_dot(value, select):
    high = value.astype(bf16).astype(f32)
    rest = value - high
    mid = rest.astype(bf16).astype(f32)
    low = rest - mid
    row = lax.broadcasted_iota(jnp.int32, (8, value.shape[1]), 0)
    stack = jnp.where(row == 0, high, jnp.where(row == 1, mid, jnp.where(row == 2, low, 0.0)))
    out = jnp.dot(stack.astype(bf16), select, preferred_element_type=f32)
    return (out[0:1] + out[1:2]) + out[2:3]


def merge_lse(rows, scale):
    top = jnp.max(rows, axis=0, keepdims=True)
    total = jnp.sum(jnp.exp((rows - top) * scale), axis=0, keepdims=True)
    return (top + jnp.log(total) / scale)[0]


def kernel(
    sizes, tok_ref, pat_ref, cnt_ref, pos_ref, loss_ref, qg_ref, pg_ref,
    zbuf, zflat, gbuf, pbuf, bias, ptran, cbuf, ebuf, coef, mbuf, lbuf, erbuf, rbuf,
    softz, softx, lossbuf, sendbuf, ownbuf, recvbuf, zsum, zsend, zrecv, pgsend, pgrecv,
    local_sem, core_send, core_recv, z_send, z_recv, g_send, g_recv, l_send, l_recv,
    s_send, s_recv, x_send, x_recv, r_send, r_recv, q_send, q_recv,
):
    NX, NY, NZ = sizes
    lanes_q = NX * NZ
    query_len = tok_ref.shape[1]
    part = query_len // NY
    group = part * lanes_q
    slab = pat_ref.shape[1]
    inv_tau = 1.0 / smooth_tau
    chunk = min(lane_chunk, group)
    wide = 2 * lanes_q

    me = lax.axis_index("pages")
    y = lax.axis_index("queries")
    core = lax.rem(me, 2)
    chip = lax.div(me, 2)
    z = lax.rem(chip, NZ)
    x = lax.div(chip, NZ)

    def device(xx, yy, zz, cc):
        return ((xx * NZ + zz) * 2 + cc, yy)

    def along(pos, step, count):
        return lax.rem(pos + step, count)

    partner = device(x, y, z, 1 - core)
    z_steps = ring_offsets(NZ)[1:]
    y_steps = ring_offsets(NY)
    xy_steps = [(dx, dy) for dy in y_steps for dx in ring_offsets(NX) if (dx, dy) != (0, 0)]

    def remote(src, dst, ssem, rsem, target):
        return pltpu.make_async_remote_copy(
            src_ref=src, dst_ref=dst, send_sem=ssem, recv_sem=rsem,
            device_id=target, device_id_type=MESH,
        )

    barrier = pltpu.get_barrier_semaphore()

    def greet(target):
        pl.semaphore_signal(barrier, inc=1, device_id=target, device_id_type=MESH)

    for d in reversed(z_steps):
        greet(device(x, y, along(z, d, NZ), core))
    for dx, dy in xy_steps:
        greet(device(along(x, dx, NX), along(y, dy, NY), z, core))
    greet(partner)

    my_tokens = tok_ref.at[0, pl.ds(pl.multiple_of(y * part, part), part), :]
    own_pages = pl.ds(core * 2, 2)
    own_tokens = pltpu.make_async_copy(my_tokens, zbuf.at[z], local_sem.at[0])
    own_tokens.start()
    own_patches = pltpu.make_async_copy(pat_ref, pbuf.at[own_pages], local_sem.at[1])
    own_patches.start()
    for i in range(2):
        cbuf[core, pl.ds(i, 1), :] = jnp.full((1, cbuf.shape[2]), cnt_ref[i], jnp.int32).astype(f32)

    pl.semaphore_wait(barrier, len(z_steps) + len(xy_steps) + 1)

    z_copies = []
    for d in reversed(z_steps):
        copy = remote(
            my_tokens, zbuf.at[z], z_send.at[d], z_recv.at[d], device(x, y, along(z, d, NZ), core)
        )
        copy.start()
        z_copies.append(copy)
    swap_patches = remote(
        pat_ref, pbuf.at[own_pages], core_send.at[0], core_recv.at[0], partner
    )
    swap_patches.start()
    swap_counts = remote(cbuf.at[core], cbuf.at[core], core_send.at[1], core_recv.at[1], partner)
    swap_counts.start()

    own_patches.wait()
    swap_counts.wait_recv()
    swap_patches.wait_recv()
    depth = pbuf.shape[2]
    slot = y * slab + lax.broadcasted_iota(jnp.int32, (slab, depth), 0)
    first_lane = lax.broadcasted_iota(jnp.int32, (slab, depth), 1) == 0
    for p in range(4):
        count = cbuf[p // 2, pl.ds(p % 2, 1), :].astype(jnp.int32)
        dead = jnp.logical_and(slot >= count, first_lane)
        bias[p] = jnp.where(dead, neg_large, 0.0).astype(bf16)
        ptran[:, p * slab : (p + 1) * slab] = pbuf[p].astype(f32).T.astype(bf16)
    select = (
        lax.broadcasted_iota(jnp.int32, (2 * lanes_q, wide), 0)
        == 2 * lax.rem(lax.broadcasted_iota(jnp.int32, (2 * lanes_q, wide), 1), lanes_q) + core
    )
    positive = jnp.dot(
        jnp.broadcast_to(pos_ref[...].astype(f32), (8, 2 * lanes_q)).astype(bf16),
        select.astype(bf16), preferred_element_type=f32,
    )[0:1]
    log_count = smooth_tau * jnp.log(
        jnp.concatenate([cbuf[0, 0:2, 0:wide], cbuf[1, 0:2, 0:wide]], axis=0)
    )

    own_tokens.wait()
    for copy in z_copies:
        copy.wait_recv()
    zflat[...] = zbuf[...].astype(f32).reshape(zflat.shape)
    for t in range(part):
        gbuf[y * part + t, x] = zflat[pl.ds(t, NZ, stride=part), :].astype(bf16)

    g_copies = {}
    mine = gbuf.at[pl.ds(y * part, part), x]
    for n, (dx, dy) in enumerate(xy_steps):
        copy = remote(
            mine, mine, g_send.at[n], g_recv.at[n],
            device(along(x, dx, NX), along(y, dy, NY), z, core),
        )
        copy.start()
        g_copies[dx, dy] = copy

    ones = jnp.where(lax.broadcasted_iota(jnp.int32, (chunk, depth), 1) == 0, 1.0, 0.0).astype(bf16)
    rows_t = chunk // lanes_q
    l_copies = []
    for k, back in enumerate(y_steps):
        for dx in range(NX):
            if (dx, back) in g_copies:
                g_copies[dx, back].wait_recv()
        gy = along(y, NY - back, NY)

        def forward(step, carry):
            p = lax.div(step, group // chunk)
            piece = lax.rem(step, group // chunk)
            tokens = gbuf[pl.ds(gy * part + piece * rows_t, rows_t)].reshape(chunk, depth)
            similar = lax.dot_general(
                jnp.concatenate([pbuf[p], bias[p]], axis=1),
                jnp.concatenate([tokens, ones], axis=1),
                (((1,), (1,)), ((), ())), preferred_element_type=f32,
            )
            top = jnp.max(similar, axis=0, keepdims=True)
            terms = jnp.exp((similar - top) * inv_tau)
            lanes = pl.ds(pl.multiple_of(piece * chunk, chunk), chunk)
            ebuf[gy, p, :, lanes] = terms
            total = jnp.sum(terms, axis=0, keepdims=True)
            mbuf[gy, pl.ds(p, 1), lanes] = top
            lbuf[y, gy, pl.ds(p, 1), lanes] = top + smooth_tau * jnp.log(total)
            return carry

        lax.fori_loop(0, 4 * (group // chunk), forward, 0)
        for n, dy in enumerate(y_steps[1:]):
            copy = remote(
                lbuf.at[y, gy], lbuf.at[y, gy], l_send.at[k, n], l_recv.at[k, n],
                device(x, along(y, dy, NY), z, core),
            )
            copy.start()
            l_copies.append(copy)

    for copy in l_copies:
        copy.wait_recv()
    sums = jnp.zeros((4, wide), f32)
    for g in range(NY):
        lse = merge_lse(lbuf[:, g], inv_tau)
        erbuf[g] = jnp.exp((mbuf[g] - lse) * inv_tau)
        for i in range(group // wide):
            sums = sums + lse[:, i * wide : (i + 1) * wide]
    sums = sums + pltpu.roll(sums, lanes_q, 1)
    logits = (sums - query_len * log_count) / page_temp
    page_id = (chip * 4 + lax.broadcasted_iota(jnp.int32, (4, wide), 0)).astype(f32)
    is_positive = page_id == positive

    softz[z, 0:1, :] = merge_lse(logits[:, None, :], 1.0)
    softz[z, 1:2, :] = jnp.sum(jnp.where(is_positive, logits, 0.0), axis=0, keepdims=True)
    s_copies = []
    for d in reversed(z_steps):
        copy = remote(
            softz.at[z], softz.at[z], s_send.at[d], s_recv.at[d],
            device(x, y, along(z, d, NZ), core),
        )
        copy.start()
        s_copies.append(copy)
    for copy in s_copies:
        copy.wait_recv()
    softx[x, 0:1, :] = merge_lse(softz[:, 0:1, :], 1.0)
    softx[x, 1:2, :] = jnp.sum(softz[:, 1:2, :], axis=0)
    x_copies = []
    for d in ring_offsets(NX)[1:]:
        copy = remote(
            softx.at[x], softx.at[x], x_send.at[d], x_recv.at[d],
            device(along(x, d, NX), y, z, core),
        )
        copy.start()
        x_copies.append(copy)
    for copy in x_copies:
        copy.wait_recv()
    all_lse = merge_lse(softx[:, 0:1, :], 1.0)
    lossbuf[core] = all_lse - jnp.sum(softx[:, 1:2, :], axis=0)
    swap_loss = remote(lossbuf.at[core], lossbuf.at[core], core_send.at[2], core_recv.at[2], partner)
    swap_loss.start()
    weights = (jnp.exp(logits - all_lse) - is_positive.astype(f32)) / page_temp
    wide_weights = jnp.concatenate([weights] * (group // wide), axis=1)
    for g in range(NY):
        rbuf[g] = erbuf[g] * wide_weights

    r_copies = []
    for back in reversed(y_steps):
        gy = along(y, NY - back, NY)

        def backward(p, carry):
            coef[gy, p] = (ebuf[gy, p] * rbuf[gy, pl.ds(p, 1), :]).astype(bf16)
            return carry

        lax.fori_loop(0, 4, backward, 0)

        def grads(piece, carry):
            lanes = pl.ds(pl.multiple_of(piece * chunk, chunk), chunk)
            across = jnp.dot(
                ptran[...], coef[gy, :, :, lanes].reshape(4 * slab, chunk),
                preferred_element_type=f32,
            )
            rows = across.T.reshape(rows_t, NX, NZ, depth)
            sendbuf[pl.ds(gy * part + piece * rows_t, rows_t)] = rows.astype(bf16)
            if back == 0:
                ownbuf[pl.ds(piece * rows_t, rows_t)] = rows
            return carry

        lax.fori_loop(0, group // chunk, grads, 0)
        for dx in range(NX):
            dy = (NY - back) % NY
            if (dx, dy) == (0, 0):
                continue
            n = xy_steps.index((dx, dy))
            xx = along(x, dx, NX)
            copy = remote(
                sendbuf.at[pl.ds(gy * part, part), xx], recvbuf.at[x * NY + y],
                r_send.at[n], r_recv.at[n], device(xx, gy, z, core),
            )
            copy.start()
            r_copies.append((copy, dx, dy))

    def page_part(p):
        total = jnp.zeros((slab, depth), f32)
        for g in range(NY):
            tokens = gbuf[g * part : (g + 1) * part].reshape(group, depth)
            total = total + jnp.dot(coef[g, p], tokens, preferred_element_type=f32)
        return total

    def other_pages(i, carry):
        pgsend[i] = page_part(2 * (1 - core) + i)
        return carry

    lax.fori_loop(0, 2, other_pages, 0)
    swap_grads = remote(pgsend, pgrecv, core_send.at[3], core_recv.at[3], partner)
    swap_grads.start()

    total = ownbuf[:, pl.ds(x, 1)].reshape(part * NZ, depth)
    for copy, dx, dy in r_copies:
        copy.wait_recv()
        source = along(x, NX - dx, NX) * NY + along(y, NY - dy, NY)
        total = total + recvbuf[source].astype(f32).reshape(part * NZ, depth)
    zsum[...] = total
    for zz in range(NZ):
        zsend[zz] = zsum[pl.ds(zz, part, stride=NZ), :]
    q_copies = []
    for d in reversed(z_steps):
        zz = along(z, d, NZ)
        copy = remote(
            zsend.at[zz], zrecv.at[z], q_send.at[d], q_recv.at[d], device(x, y, zz, core)
        )
        copy.start()
        q_copies.append((copy, d))

    def own_page(i, carry):
        pg_ref[i] = page_part(2 * core + i)
        return carry

    lax.fori_loop(0, 2, own_page, 0)
    swap_grads.wait_recv()
    pg_ref[...] += pgrecv[...]

    swap_loss.wait_recv()
    row = lax.broadcasted_iota(jnp.int32, (wide, 2 * lanes_q), 0)
    col = lax.broadcasted_iota(jnp.int32, (wide, 2 * lanes_q), 1)
    loss = jnp.zeros((1, 2 * lanes_q), f32)
    for c in range(2):
        spread = jnp.logical_and(col == 2 * row + c, row < lanes_q).astype(f32).astype(bf16)
        loss = loss + onehot_dot(lossbuf[c], spread)
    loss_ref[...] = loss

    total = zsend[z]
    for copy, d in q_copies:
        copy.wait_recv()
        total = total + zrecv[along(z, NZ - d, NZ)]
    qg_ref[0] = total

    for copy in z_copies + list(g_copies.values()) + l_copies + s_copies + x_copies:
        copy.wait_send()
    for copy in [swap_patches, swap_counts, swap_loss, swap_grads]:
        copy.wait_send()
    for copy, *_ in r_copies + q_copies:
        copy.wait_send()


def shards(sizes, query_tokens, page_patches, patch_counts, positive_page):
    NX, NY, NZ = sizes
    _, query_len, depth = query_tokens.shape
    slab = page_patches.shape[1]
    part = query_len // NY
    lanes_q = NX * NZ
    group = part * lanes_q
    wide = 2 * lanes_q
    peers = NX * NY - 1
    vmem = pltpu.VMEM
    dma = pltpu.SemaphoreType.DMA
    loss, query_grad, page_grad = pl.pallas_call(
        functools.partial(kernel, sizes),
        out_shape=(
            jax.ShapeDtypeStruct((1, 2 * lanes_q), f32),
            jax.ShapeDtypeStruct((1, part, depth), f32),
            jax.ShapeDtypeStruct((2, slab, depth), f32),
        ),
        in_specs=[
            pl.BlockSpec(memory_space=pltpu.VMEM),
            pl.BlockSpec(memory_space=pltpu.VMEM),
            pl.BlockSpec(memory_space=pltpu.SMEM),
            pl.BlockSpec(memory_space=pltpu.VMEM),
        ],
        out_specs=[pl.BlockSpec(memory_space=pltpu.VMEM)] * 3,
        scratch_shapes=[
            vmem((NZ, part, depth), bf16),
            vmem((NZ * part, depth), f32),
            vmem((query_len, NX, NZ, depth), bf16),
            vmem((4, slab, depth), bf16),
            vmem((4, slab, depth), bf16),
            vmem((depth, 4 * slab), bf16),
            vmem((2, 8, depth), f32),
            vmem((NY, 4, slab, group), f32),
            vmem((NY, 4, slab, group), bf16),
            vmem((NY, 4, group), f32),
            vmem((NY, NY, 4, group), f32),
            vmem((NY, 4, group), f32),
            vmem((NY, 4, group), f32),
            vmem((NZ, 2, wide), f32),
            vmem((NX, 2, wide), f32),
            vmem((2, 1, wide), f32),
            vmem((query_len, NX, NZ, depth), bf16),
            vmem((part, NX, NZ, depth), f32),
            vmem((NX * NY, part, NZ, depth), bf16),
            vmem((part * NZ, depth), f32),
            vmem((NZ, part, depth), f32),
            vmem((NZ, part, depth), f32),
            vmem((2, slab, depth), f32),
            vmem((2, slab, depth), f32),
            dma((2,)),
            dma((4,)), dma((4,)),
            dma((NZ,)), dma((NZ,)),
            dma((peers,)), dma((peers,)),
            dma((NY, NY - 1)), dma((NY, NY - 1)),
            dma((NZ,)), dma((NZ,)),
            dma((NX,)), dma((NX,)),
            dma((peers,)), dma((peers,)),
            dma((NZ,)), dma((NZ,)),
        ],
        compiler_params=pltpu.CompilerParams(
            collective_id=0, has_side_effects=True, vmem_limit_bytes=56 * 1024 * 1024
        ),
    )(query_tokens, page_patches, patch_counts, positive_page.reshape(1, 2 * lanes_q))
    return (loss.reshape(2 * lanes_q), query_grad, page_grad)


def solution(mesh):
    chips = mesh.shape["pages"] // 2
    sizes = (chips // chips_z, mesh.shape["queries"], chips_z)
    in_specs = (P("pages", None, None), P("pages", "queries", None), P("pages"), P())
    out_specs = (P(), P("pages", "queries", None), P("pages", "queries", None))
    return jax.shard_map(
        functools.partial(shards, sizes),
        mesh=mesh, in_specs=in_specs, out_specs=out_specs, check_vma=False,
    )
```

```python
import functools
import math

import jax
import jax.numpy as jnp
from jax import lax
from jax.experimental import pallas as pl
from jax.experimental.pallas import tpu as pltpu
from jax.sharding import PartitionSpec as P

smooth_tau = 0.05
page_temp = 0.02
neg_large = -1e30
chips_z = 16
lane_chunk = 256
MESH = pl.DeviceIdType.MESH
f32, bf16 = jnp.float32, jnp.bfloat16


def ring_offsets(count):
    near = sorted(range(count), key=lambda d: (min(d, count - d), d))
    return near


def onehot_dot(value, select):
    high = value.astype(bf16).astype(f32)
    rest = value - high
    mid = rest.astype(bf16).astype(f32)
    low = rest - mid
    row = lax.broadcasted_iota(jnp.int32, (8, value.shape[1]), 0)
    stack = jnp.where(row == 0, high, jnp.where(row == 1, mid, jnp.where(row == 2, low, 0.0)))
    out = jnp.dot(stack.astype(bf16), select, preferred_element_type=f32)
    return (out[0:1] + out[1:2]) + out[2:3]


def merge_lse(rows, scale):
    top = jnp.max(rows, axis=0, keepdims=True)
    total = jnp.sum(jnp.exp((rows - top) * scale), axis=0, keepdims=True)
    return (top + jnp.log(total) / scale)[0]


def kernel(
    sizes, tok_ref, pat_ref, cnt_ref, pos_ref, loss_ref, qg_ref, pg_ref,
    counts, pos_row, loss_row, qg_tile, pg_tile,
    zbuf, zflat, gbuf, pbuf, bias, ptran, cbuf, ebuf, coef, mbuf, lbuf, erbuf, rbuf,
    held_a, held_b, softz, softx, lossbuf, sendbuf, ownbuf, recvbuf, zsum, zsend, zrecv, pgsend, pgrecv,
    local_sem, core_send, core_recv, z_send, z_recv, g_send, g_recv, l_send, l_recv,
    s_send, s_recv, x_send, x_recv, r_send, r_recv, q_send, q_recv,
):
    NX, NY, NZ = sizes
    lanes_q = NX * NZ
    query_len = tok_ref.shape[1]
    part = query_len // NY
    group = part * lanes_q
    slab = pat_ref.shape[1]
    held = (held_a, held_b)
    inv_tau = 1.0 / smooth_tau
    exp_scale = inv_tau * math.log2(math.e)
    chunk = min(lane_chunk, group)
    wide = 2 * lanes_q

    me = lax.axis_index("pages")
    y = lax.axis_index("queries")
    core = lax.rem(me, 2)
    chip = lax.div(me, 2)
    z = lax.rem(chip, NZ)
    x = lax.div(chip, NZ)

    def device(xx, yy, zz, cc):
        return ((xx * NZ + zz) * 2 + cc, yy)

    def along(pos, step, count):
        return lax.rem(pos + step, count)

    partner = device(x, y, z, 1 - core)
    z_steps = ring_offsets(NZ)[1:]
    y_steps = ring_offsets(NY)
    xy_steps = [(dx, dy) for dy in y_steps for dx in ring_offsets(NX) if (dx, dy) != (0, 0)]

    def remote(src, dst, ssem, rsem, target):
        return pltpu.make_async_remote_copy(
            src_ref=src, dst_ref=dst, send_sem=ssem, recv_sem=rsem,
            device_id=target, device_id_type=MESH,
        )

    barrier = pltpu.get_barrier_semaphore()

    def greet(target):
        pl.semaphore_signal(barrier, inc=1, device_id=target, device_id_type=MESH)

    for d in reversed(z_steps):
        greet(device(x, y, along(z, d, NZ), core))
    for dx, dy in xy_steps:
        greet(device(along(x, dx, NX), along(y, dy, NY), z, core))
    greet(partner)

    my_tokens = tok_ref.at[0, pl.ds(pl.multiple_of(y * part, part), part), :]
    own_pages = pl.ds(core * 2, 2)
    own_counts = pltpu.make_async_copy(cnt_ref, counts, local_sem.at[2])
    own_counts.start()
    own_pos = pltpu.make_async_copy(pos_ref, pos_row, local_sem.at[3])
    own_pos.start()
    own_tokens = pltpu.make_async_copy(my_tokens, zbuf.at[z], local_sem.at[0])
    own_tokens.start()
    own_patches = pltpu.make_async_copy(pat_ref, pbuf.at[own_pages], local_sem.at[1])
    own_patches.start()
    own_counts.wait()
    for i in range(2):
        cbuf[core, pl.ds(i, 1), :] = jnp.full((1, cbuf.shape[2]), counts[i], jnp.int32).astype(f32)

    pl.semaphore_wait(barrier, len(z_steps) + len(xy_steps) + 1)

    z_copies = []
    for d in reversed(z_steps):
        copy = remote(
            my_tokens, zbuf.at[z], z_send.at[d], z_recv.at[d], device(x, y, along(z, d, NZ), core)
        )
        copy.start()
        z_copies.append(copy)
    swap_patches = remote(
        pat_ref, pbuf.at[own_pages], core_send.at[0], core_recv.at[0], partner
    )
    swap_patches.start()
    swap_counts = remote(cbuf.at[core], cbuf.at[core], core_send.at[1], core_recv.at[1], partner)
    swap_counts.start()

    own_patches.wait()
    swap_counts.wait_recv()
    swap_patches.wait_recv()
    depth = pbuf.shape[2]
    slot = y * slab + lax.broadcasted_iota(jnp.int32, (slab, depth), 0)
    first_lane = lax.broadcasted_iota(jnp.int32, (slab, depth), 1) == 0
    for p in range(4):
        count = cbuf[p // 2, pl.ds(p % 2, 1), :].astype(jnp.int32)
        dead = jnp.logical_and(slot >= count, first_lane)
        bias[p] = jnp.where(dead, neg_large, 0.0).astype(bf16)
        ptran[:, p * slab : (p + 1) * slab] = pbuf[p].astype(f32).T.astype(bf16)
    select = (
        lax.broadcasted_iota(jnp.int32, (2 * lanes_q, wide), 0)
        == 2 * lax.rem(lax.broadcasted_iota(jnp.int32, (2 * lanes_q, wide), 1), lanes_q) + core
    )
    own_pos.wait()
    positive = jnp.dot(
        jnp.broadcast_to(pos_row[...].astype(f32), (8, 2 * lanes_q)).astype(bf16),
        select.astype(bf16), preferred_element_type=f32,
    )[0:1]
    log_count = smooth_tau * jnp.log(
        jnp.concatenate([cbuf[0, 0:2, 0:wide], cbuf[1, 0:2, 0:wide]], axis=0)
    )

    own_tokens.wait()
    for copy in z_copies:
        copy.wait_recv()
    zflat[...] = zbuf[...].astype(f32).reshape(zflat.shape)
    for t in range(part):
        gbuf[y * part + t, x] = zflat[pl.ds(t, NZ, stride=part), :].astype(bf16)

    g_copies = {}
    mine = gbuf.at[pl.ds(y * part, part), x]
    for n, (dx, dy) in enumerate(xy_steps):
        copy = remote(
            mine, mine, g_send.at[n], g_recv.at[n],
            device(along(x, dx, NX), along(y, dy, NY), z, core),
        )
        copy.start()
        g_copies[dx, dy] = copy

    ones = jnp.where(lax.broadcasted_iota(jnp.int32, (chunk, depth), 1) == 0, 1.0, 0.0).astype(bf16)
    rows_t = chunk // lanes_q
    l_copies = []
    for k, back in enumerate(y_steps):
        for dx in range(NX):
            if (dx, back) in g_copies:
                g_copies[dx, back].wait_recv()
        gy = along(y, NY - back, NY)

        def scores(block):
            p, piece = block % 4, block // 4
            tokens = gbuf[pl.ds(gy * part + piece * rows_t, rows_t)].reshape(chunk, depth)
            similar = lax.dot_general(
                jnp.concatenate([pbuf[p], bias[p]], axis=1),
                jnp.concatenate([tokens, ones], axis=1),
                (((1,), (1,)), ((), ())), preferred_element_type=f32,
            )
            held[block % 2][...] = similar
            return jnp.max(similar, axis=0, keepdims=True)

        def exponents(block, top):
            p, piece = block % 4, block // 4
            lanes = slice(piece * chunk, (piece + 1) * chunk)
            terms = jnp.exp2((held[block % 2][...] - top) * exp_scale)
            ebuf[gy, p, :, lanes] = terms
            total = jnp.sum(terms, axis=0, keepdims=True)
            mbuf[gy, p : p + 1, lanes] = top
            lbuf[y, gy, p : p + 1, lanes] = top + smooth_tau * jnp.log(total)

        blocks = 4 * (group // chunk)
        top = scores(0)
        for block in range(blocks):
            following = scores(block + 1) if block + 1 < blocks else None
            exponents(block, top)
            top = following
        for n, dy in enumerate(y_steps[1:]):
            copy = remote(
                lbuf.at[y, gy], lbuf.at[y, gy], l_send.at[k, n], l_recv.at[k, n],
                device(x, along(y, dy, NY), z, core),
            )
            copy.start()
            l_copies.append(copy)

    for copy in l_copies:
        copy.wait_recv()
    sums = jnp.zeros((4, wide), f32)
    for g in range(NY):
        lse = merge_lse(lbuf[:, g], inv_tau)
        erbuf[g] = jnp.exp((mbuf[g] - lse) * inv_tau)
        for i in range(group // wide):
            sums = sums + lse[:, i * wide : (i + 1) * wide]
    sums = sums + pltpu.roll(sums, lanes_q, 1)
    logits = (sums - query_len * log_count) / page_temp
    page_id = (chip * 4 + lax.broadcasted_iota(jnp.int32, (4, wide), 0)).astype(f32)
    is_positive = page_id == positive

    softz[z, 0:1, :] = merge_lse(logits[:, None, :], 1.0)
    softz[z, 1:2, :] = jnp.sum(jnp.where(is_positive, logits, 0.0), axis=0, keepdims=True)
    s_copies = []
    for d in reversed(z_steps):
        copy = remote(
            softz.at[z], softz.at[z], s_send.at[d], s_recv.at[d],
            device(x, y, along(z, d, NZ), core),
        )
        copy.start()
        s_copies.append(copy)
    for copy in s_copies:
        copy.wait_recv()
    softx[x, 0:1, :] = merge_lse(softz[:, 0:1, :], 1.0)
    softx[x, 1:2, :] = jnp.sum(softz[:, 1:2, :], axis=0)
    x_copies = []
    for d in ring_offsets(NX)[1:]:
        copy = remote(
            softx.at[x], softx.at[x], x_send.at[d], x_recv.at[d],
            device(along(x, d, NX), y, z, core),
        )
        copy.start()
        x_copies.append(copy)
    for copy in x_copies:
        copy.wait_recv()
    all_lse = merge_lse(softx[:, 0:1, :], 1.0)
    lossbuf[core] = all_lse - jnp.sum(softx[:, 1:2, :], axis=0)
    swap_loss = remote(lossbuf.at[core], lossbuf.at[core], core_send.at[2], core_recv.at[2], partner)
    swap_loss.start()
    weights = (jnp.exp(logits - all_lse) - is_positive.astype(f32)) / page_temp
    wide_weights = jnp.concatenate([weights] * (group // wide), axis=1)
    for g in range(NY):
        rbuf[g] = erbuf[g] * wide_weights

    r_copies = []
    for back in reversed(y_steps):
        gy = along(y, NY - back, NY)

        def backward(p, carry):
            coef[gy, p] = (ebuf[gy, p] * rbuf[gy, pl.ds(p, 1), :]).astype(bf16)
            return carry

        lax.fori_loop(0, 4, backward, 0)

        def grads(piece, carry):
            lanes = pl.ds(pl.multiple_of(piece * chunk, chunk), chunk)
            across = jnp.dot(
                ptran[...], coef[gy, :, :, lanes].reshape(4 * slab, chunk),
                preferred_element_type=f32,
            )
            rows = across.T.reshape(rows_t, NX, NZ, depth)
            sendbuf[pl.ds(gy * part + piece * rows_t, rows_t)] = rows.astype(bf16)
            if back == 0:
                ownbuf[pl.ds(piece * rows_t, rows_t)] = rows
            return carry

        lax.fori_loop(0, group // chunk, grads, 0)
        for dx in range(NX):
            dy = (NY - back) % NY
            if (dx, dy) == (0, 0):
                continue
            n = xy_steps.index((dx, dy))
            xx = along(x, dx, NX)
            copy = remote(
                sendbuf.at[pl.ds(gy * part, part), xx], recvbuf.at[x * NY + y],
                r_send.at[n], r_recv.at[n], device(xx, gy, z, core),
            )
            copy.start()
            r_copies.append((copy, dx, dy))

    def page_part(p):
        total = jnp.zeros((slab, depth), f32)
        for g in range(NY):
            tokens = gbuf[g * part : (g + 1) * part].reshape(group, depth)
            total = total + jnp.dot(coef[g, p], tokens, preferred_element_type=f32)
        return total

    def other_pages(i, carry):
        pgsend[i] = page_part(2 * (1 - core) + i)
        return carry

    lax.fori_loop(0, 2, other_pages, 0)
    swap_grads = remote(pgsend, pgrecv, core_send.at[3], core_recv.at[3], partner)
    swap_grads.start()

    total = ownbuf[:, pl.ds(x, 1)].reshape(part * NZ, depth)
    for copy, dx, dy in r_copies:
        copy.wait_recv()
        source = along(x, NX - dx, NX) * NY + along(y, NY - dy, NY)
        total = total + recvbuf[source].astype(f32).reshape(part * NZ, depth)
    zsum[...] = total
    for zz in range(NZ):
        zsend[zz] = zsum[pl.ds(zz, part, stride=NZ), :]
    q_copies = []
    for d in reversed(z_steps):
        zz = along(z, d, NZ)
        copy = remote(
            zsend.at[zz], zrecv.at[z], q_send.at[d], q_recv.at[d], device(x, y, zz, core)
        )
        copy.start()
        q_copies.append((copy, d))

    def own_page(i, carry):
        pg_tile[i] = page_part(2 * core + i)
        return carry

    lax.fori_loop(0, 2, own_page, 0)
    swap_grads.wait_recv()
    pg_tile[...] += pgrecv[...]
    outs = [pltpu.make_async_copy(pg_tile, pg_ref, local_sem.at[4])]
    outs[0].start()

    swap_loss.wait_recv()
    row = lax.broadcasted_iota(jnp.int32, (wide, 2 * lanes_q), 0)
    col = lax.broadcasted_iota(jnp.int32, (wide, 2 * lanes_q), 1)
    loss = jnp.zeros((1, 2 * lanes_q), f32)
    for c in range(2):
        spread = jnp.logical_and(col == 2 * row + c, row < lanes_q).astype(f32).astype(bf16)
        loss = loss + onehot_dot(lossbuf[c], spread)
    loss_row[...] = loss
    outs.append(pltpu.make_async_copy(loss_row, loss_ref, local_sem.at[5]))
    outs[1].start()

    total = zsend[z]
    for copy, d in q_copies:
        copy.wait_recv()
        total = total + zrecv[along(z, NZ - d, NZ)]
    qg_tile[0] = total
    outs.append(pltpu.make_async_copy(qg_tile, qg_ref, local_sem.at[6]))
    outs[2].start()

    for copy in z_copies + list(g_copies.values()) + l_copies + s_copies + x_copies:
        copy.wait_send()
    for copy in [swap_patches, swap_counts, swap_loss, swap_grads]:
        copy.wait_send()
    for copy, *_ in r_copies + q_copies:
        copy.wait_send()
    for copy in outs:
        copy.wait()


def hand_on(*refs):
    sources, targets, tiles, sem = refs[:3], refs[3:6], refs[6:9], refs[9]
    takes = [pltpu.make_async_copy(s, t, sem.at[i]) for i, (s, t) in enumerate(zip(sources, tiles))]
    gives = [pltpu.make_async_copy(t, o, sem.at[i]) for i, (t, o) in enumerate(zip(tiles, targets))]
    for copy in takes:
        copy.start()
    for take, give in zip(takes, gives):
        take.wait()
        give.start()
    for copy in gives:
        copy.wait()


def shards(sizes, query_tokens, page_patches, patch_counts, positive_page):
    NX, NY, NZ = sizes
    _, query_len, depth = query_tokens.shape
    slab = page_patches.shape[1]
    part = query_len // NY
    lanes_q = NX * NZ
    group = part * lanes_q
    wide = 2 * lanes_q
    peers = NX * NY - 1
    vmem = pltpu.VMEM
    dma = pltpu.SemaphoreType.DMA
    shapes = [
        jax.ShapeDtypeStruct((2, slab, depth), f32),
        jax.ShapeDtypeStruct((1, part, depth), f32),
        jax.ShapeDtypeStruct((1, 2 * lanes_q), f32),
    ]
    hbm = pl.BlockSpec(memory_space=pltpu.HBM)
    loss, query_grad, page_grad = pl.pallas_call(
        functools.partial(kernel, sizes),
        out_shape=shapes[::-1],
        in_specs=[hbm] * 4,
        out_specs=[hbm] * 3,
        scratch_shapes=[
            pltpu.SMEM((2,), jnp.int32),
            vmem((1, 2 * lanes_q), jnp.int32),
            vmem((1, 2 * lanes_q), f32),
            vmem((1, part, depth), f32),
            vmem((2, slab, depth), f32),
            vmem((NZ, part, depth), bf16),
            vmem((NZ * part, depth), f32),
            vmem((query_len, NX, NZ, depth), bf16),
            vmem((4, slab, depth), bf16),
            vmem((4, slab, depth), bf16),
            vmem((depth, 4 * slab), bf16),
            vmem((2, 8, depth), f32),
            vmem((NY, 4, slab, group), f32),
            vmem((NY, 4, slab, group), bf16),
            vmem((NY, 4, group), f32),
            vmem((NY, NY, 4, group), f32),
            vmem((NY, 4, group), f32),
            vmem((NY, 4, group), f32),
            vmem((slab, min(lane_chunk, group)), f32),
            vmem((slab, min(lane_chunk, group)), f32),
            vmem((NZ, 2, wide), f32),
            vmem((NX, 2, wide), f32),
            vmem((2, 1, wide), f32),
            vmem((query_len, NX, NZ, depth), bf16),
            vmem((part, NX, NZ, depth), f32),
            vmem((NX * NY, part, NZ, depth), bf16),
            vmem((part * NZ, depth), f32),
            vmem((NZ, part, depth), f32),
            vmem((NZ, part, depth), f32),
            vmem((2, slab, depth), f32),
            vmem((2, slab, depth), f32),
            dma((7,)),
            dma((4,)), dma((4,)),
            dma((NZ,)), dma((NZ,)),
            dma((peers,)), dma((peers,)),
            dma((NY, NY - 1)), dma((NY, NY - 1)),
            dma((NZ,)), dma((NZ,)),
            dma((NX,)), dma((NX,)),
            dma((peers,)), dma((peers,)),
            dma((NZ,)), dma((NZ,)),
        ],
        compiler_params=pltpu.CompilerParams(
            collective_id=0, has_side_effects=True, vmem_limit_bytes=56 * 1024 * 1024
        ),
    )(query_tokens, page_patches, patch_counts, positive_page.reshape(1, 2 * lanes_q))
    page_grad, query_grad, loss = pl.pallas_call(
        hand_on,
        out_shape=shapes,
        in_specs=[hbm] * 3,
        out_specs=[hbm] * 3,
        scratch_shapes=[vmem(shape.shape, f32) for shape in shapes] + [dma((3,))],
    )(page_grad, query_grad, loss)
    return (loss.reshape(2 * lanes_q), query_grad, page_grad)


def solution(mesh):
    chips = mesh.shape["pages"] // 2
    sizes = (chips // chips_z, mesh.shape["queries"], chips_z)
    in_specs = (P("pages", None, None), P("pages", "queries", None), P("pages"), P())
    out_specs = (P(), P("pages", "queries", None), P("pages", "queries", None))
    return jax.shard_map(
        functools.partial(shards, sizes),
        mesh=mesh, in_specs=in_specs, out_specs=out_specs, check_vma=False,
    )
```

```python
import functools
import math

import jax
import jax.numpy as jnp
from jax import lax
from jax.experimental import pallas as pl
from jax.experimental.pallas import tpu as pltpu
from jax.sharding import PartitionSpec as P

smooth_tau = 0.05
page_temp = 0.02
neg_large = -1e30
chips_z = 16
lane_chunk = 256
MESH = pl.DeviceIdType.MESH
f32, bf16 = jnp.float32, jnp.bfloat16


def ring_offsets(count):
    near = sorted(range(count), key=lambda d: (min(d, count - d), d))
    return near


def onehot_dot(value, select):
    high = value.astype(bf16).astype(f32)
    rest = value - high
    mid = rest.astype(bf16).astype(f32)
    low = rest - mid
    row = lax.broadcasted_iota(jnp.int32, (8, value.shape[1]), 0)
    stack = jnp.where(row == 0, high, jnp.where(row == 1, mid, jnp.where(row == 2, low, 0.0)))
    out = jnp.dot(stack.astype(bf16), select, preferred_element_type=f32)
    return (out[0:1] + out[1:2]) + out[2:3]


def merge_lse(rows, scale):
    top = jnp.max(rows, axis=0, keepdims=True)
    total = jnp.sum(jnp.exp((rows - top) * scale), axis=0, keepdims=True)
    return (top + jnp.log(total) / scale)[0]


def kernel(
    sizes, tok_ref, pat_ref, cnt_ref, pos_ref, loss_ref, qg_ref, pg_ref,
    counts, pos_row, loss_row, qg_tile, pg_tile,
    zbuf, zflat, stage, gbuf, pbuf, bias, ptran, cbuf, ebuf, coef, mbuf, lbuf, erbuf, rbuf,
    held_a, held_b, softz, softx, lossbuf, sendbuf, ownbuf, recvbuf, zsum, zsend, zrecv, pgsend, pgrecv,
    ready, local_sem, core_send, core_recv, z_send, z_recv, g_send, g_recv, l_send, l_recv,
    s_send, s_recv, x_send, x_recv, r_send, r_recv, q_send, q_recv,
):
    NX, NY, NZ = sizes
    lanes_q = NX * NZ
    query_len = tok_ref.shape[1]
    part = query_len // NY
    group = part * lanes_q
    slab = pat_ref.shape[1]
    held = (held_a, held_b)
    inv_tau = 1.0 / smooth_tau
    exp_scale = inv_tau * math.log2(math.e)
    chunk = min(lane_chunk, group)
    wide = 2 * lanes_q

    me = lax.axis_index("pages")
    y = lax.axis_index("queries")
    core = lax.rem(me, 2)
    chip = lax.div(me, 2)
    z = lax.rem(chip, NZ)
    x = lax.div(chip, NZ)

    def device(xx, yy, zz, cc):
        return ((xx * NZ + zz) * 2 + cc, yy)

    def along(pos, step, count):
        return lax.rem(pos + step, count)

    partner = device(x, y, z, 1 - core)
    z_steps = ring_offsets(NZ)[1:]
    y_steps = ring_offsets(NY)
    xy_steps = [(dx, dy) for dy in y_steps for dx in ring_offsets(NX) if (dx, dy) != (0, 0)]

    def remote(src, dst, ssem, rsem, target):
        return pltpu.make_async_remote_copy(
            src_ref=src, dst_ref=dst, send_sem=ssem, recv_sem=rsem,
            device_id=target, device_id_type=MESH,
        )

    barrier = pltpu.get_barrier_semaphore()

    def greet(target):
        pl.semaphore_signal(barrier, inc=1, device_id=target, device_id_type=MESH)

    @pl.when(core == 0)
    def _():
        for cc in range(2):
            for d in reversed(z_steps):
                greet(device(x, y, along(z, d, NZ), cc))
            for dx, dy in xy_steps:
                greet(device(along(x, dx, NX), along(y, dy, NY), z, cc))
        greet(partner)

    my_tokens = tok_ref.at[0, pl.ds(pl.multiple_of(y * part, part), part), :]
    own_pages = pl.ds(core * 2, 2)
    own_counts = pltpu.make_async_copy(cnt_ref, counts, local_sem.at[2])
    own_counts.start()
    own_pos = pltpu.make_async_copy(pos_ref, pos_row, local_sem.at[3])
    own_pos.start()
    own_tokens = pltpu.make_async_copy(my_tokens, zbuf.at[core, z], local_sem.at[0])
    own_tokens.start()
    own_patches = pltpu.make_async_copy(pat_ref, pbuf.at[own_pages], local_sem.at[1])
    own_patches.start()
    own_counts.wait()
    for i in range(2):
        cbuf[core, pl.ds(i, 1), :] = jnp.full((1, cbuf.shape[2]), counts[i], jnp.int32).astype(f32)

    pl.semaphore_wait(barrier, len(z_steps) + len(xy_steps) + core)

    @pl.when(core == 1)
    def _():
        for dx, dy in xy_steps:
            pl.semaphore_signal(
                ready, inc=1, device_id=device(along(x, dx, NX), along(y, dy, NY), z, 0),
                device_id_type=MESH,
            )

    def z_copy(source_core, d):
        return remote(
            my_tokens, zbuf.at[source_core, z], z_send.at[d], z_recv.at[source_core, d],
            device(x, y, along(z, d, NZ), 0),
        )

    for d in reversed(z_steps):
        z_copy(core, d).start()
    swap_patches = remote(
        pat_ref, pbuf.at[own_pages], core_send.at[0], core_recv.at[0], partner
    )
    swap_counts = remote(cbuf.at[core], cbuf.at[core], core_send.at[1], core_recv.at[1], partner)

    @pl.when(core == 1)
    def _():
        z_copy(1, 0).start()

    @pl.when(core == 0)
    def _():
        z_copy(1, 0).wait_recv()

    swap_patches.start()
    swap_counts.start()

    own_patches.wait()
    swap_counts.wait_recv()
    swap_patches.wait_recv()
    depth = pbuf.shape[2]
    slot = y * slab + lax.broadcasted_iota(jnp.int32, (slab, depth), 0)
    first_lane = lax.broadcasted_iota(jnp.int32, (slab, depth), 1) == 0
    for p in range(4):
        count = cbuf[p // 2, pl.ds(p % 2, 1), :].astype(jnp.int32)
        dead = jnp.logical_and(slot >= count, first_lane)
        bias[p] = jnp.where(dead, neg_large, 0.0).astype(bf16)
        ptran[:, p * slab : (p + 1) * slab] = pbuf[p].astype(f32).T.astype(bf16)
    select = (
        lax.broadcasted_iota(jnp.int32, (2 * lanes_q, wide), 0)
        == 2 * lax.rem(lax.broadcasted_iota(jnp.int32, (2 * lanes_q, wide), 1), lanes_q) + core
    )
    own_pos.wait()
    positive = jnp.dot(
        jnp.broadcast_to(pos_row[...].astype(f32), (8, 2 * lanes_q)).astype(bf16),
        select.astype(bf16), preferred_element_type=f32,
    )[0:1]
    log_count = smooth_tau * jnp.log(
        jnp.concatenate([cbuf[0, 0:2, 0:wide], cbuf[1, 0:2, 0:wide]], axis=0)
    )

    own_tokens.wait()
    mine = gbuf.at[pl.ds(y * part, part), x]

    def g_copy(source_core, dx, dy):
        n = dy * NX + dx
        return remote(
            mine if source_core == 0 else stage, mine,
            g_send.at[source_core, n], g_recv.at[n],
            device(along(x, dx, NX), along(y, dy, NY), z, source_core),
        )

    @pl.when(core == 0)
    def _():
        for d in z_steps:
            z_copy(0, d).wait_recv()
        zflat[...] = zbuf[0].astype(f32).reshape(zflat.shape)
        for t in range(part):
            gbuf[y * part + t, x] = zflat[pl.ds(t, NZ, stride=part), :].astype(bf16)
        for dx, dy in xy_steps:
            g_copy(0, dx, dy).start()
        for d in z_steps:
            z_copy(1, d).wait_recv()
        zflat[...] = zbuf[1].astype(f32).reshape(zflat.shape)
        for t in range(part):
            stage[t] = zflat[pl.ds(t, NZ, stride=part), :].astype(bf16)
        pl.semaphore_wait(ready, len(xy_steps))
        for dx, dy in [(0, 0)] + xy_steps:
            g_copy(1, dx, dy).start()

    ones = jnp.where(lax.broadcasted_iota(jnp.int32, (chunk, depth), 1) == 0, 1.0, 0.0).astype(bf16)
    rows_t = chunk // lanes_q
    l_copies = []
    for k, back in enumerate(y_steps):
        for dx in range(NX):
            if (dx, back) != (0, 0):
                g_copy(0, dx, back).wait_recv()
        if back == 0:

            @pl.when(core == 1)
            def _():
                g_copy(0, 0, 0).wait_recv()

        gy = along(y, NY - back, NY)

        def scores(block):
            p, piece = block % 4, block // 4
            tokens = gbuf[pl.ds(gy * part + piece * rows_t, rows_t)].reshape(chunk, depth)
            similar = lax.dot_general(
                jnp.concatenate([pbuf[p], bias[p]], axis=1),
                jnp.concatenate([tokens, ones], axis=1),
                (((1,), (1,)), ((), ())), preferred_element_type=f32,
            )
            held[block % 2][...] = similar
            return jnp.max(similar, axis=0, keepdims=True)

        def exponents(block, top):
            p, piece = block % 4, block // 4
            lanes = slice(piece * chunk, (piece + 1) * chunk)
            terms = jnp.exp2((held[block % 2][...] - top) * exp_scale)
            ebuf[gy, p, :, lanes] = terms
            total = jnp.sum(terms, axis=0, keepdims=True)
            mbuf[gy, p : p + 1, lanes] = top
            lbuf[y, gy, p : p + 1, lanes] = top + smooth_tau * jnp.log(total)

        blocks = 4 * (group // chunk)
        top = scores(0)
        for block in range(blocks):
            following = scores(block + 1) if block + 1 < blocks else None
            exponents(block, top)
            top = following
        for n, dy in enumerate(y_steps[1:]):
            copy = remote(
                lbuf.at[y, gy], lbuf.at[y, gy], l_send.at[k, n], l_recv.at[k, n],
                device(x, along(y, dy, NY), z, core),
            )
            copy.start()
            l_copies.append(copy)

    for copy in l_copies:
        copy.wait_recv()
    sums = jnp.zeros((4, wide), f32)
    for g in range(NY):
        lse = merge_lse(lbuf[:, g], inv_tau)
        erbuf[g] = jnp.exp((mbuf[g] - lse) * inv_tau)
        for i in range(group // wide):
            sums = sums + lse[:, i * wide : (i + 1) * wide]
    sums = sums + pltpu.roll(sums, lanes_q, 1)
    logits = (sums - query_len * log_count) / page_temp
    page_id = (chip * 4 + lax.broadcasted_iota(jnp.int32, (4, wide), 0)).astype(f32)
    is_positive = page_id == positive

    softz[z, 0:1, :] = merge_lse(logits[:, None, :], 1.0)
    softz[z, 1:2, :] = jnp.sum(jnp.where(is_positive, logits, 0.0), axis=0, keepdims=True)
    s_copies = []
    for d in reversed(z_steps):
        copy = remote(
            softz.at[z], softz.at[z], s_send.at[d], s_recv.at[d],
            device(x, y, along(z, d, NZ), core),
        )
        copy.start()
        s_copies.append(copy)
    for copy in s_copies:
        copy.wait_recv()
    softx[x, 0:1, :] = merge_lse(softz[:, 0:1, :], 1.0)
    softx[x, 1:2, :] = jnp.sum(softz[:, 1:2, :], axis=0)
    x_copies = []
    for d in ring_offsets(NX)[1:]:
        copy = remote(
            softx.at[x], softx.at[x], x_send.at[d], x_recv.at[d],
            device(along(x, d, NX), y, z, core),
        )
        copy.start()
        x_copies.append(copy)
    for copy in x_copies:
        copy.wait_recv()
    all_lse = merge_lse(softx[:, 0:1, :], 1.0)
    lossbuf[core] = all_lse - jnp.sum(softx[:, 1:2, :], axis=0)
    swap_loss = remote(lossbuf.at[core], lossbuf.at[core], core_send.at[2], core_recv.at[2], partner)
    swap_loss.start()
    weights = (jnp.exp(logits - all_lse) - is_positive.astype(f32)) / page_temp
    wide_weights = jnp.concatenate([weights] * (group // wide), axis=1)
    for g in range(NY):
        rbuf[g] = erbuf[g] * wide_weights

    r_copies = []
    for back in reversed(y_steps):
        gy = along(y, NY - back, NY)

        def backward(p, carry):
            coef[gy, p] = (ebuf[gy, p] * rbuf[gy, pl.ds(p, 1), :]).astype(bf16)
            return carry

        lax.fori_loop(0, 4, backward, 0)

        def grads(piece, carry):
            lanes = pl.ds(pl.multiple_of(piece * chunk, chunk), chunk)
            across = jnp.dot(
                ptran[...], coef[gy, :, :, lanes].reshape(4 * slab, chunk),
                preferred_element_type=f32,
            )
            rows = across.T.reshape(rows_t, NX, NZ, depth)
            sendbuf[pl.ds(gy * part + piece * rows_t, rows_t)] = rows.astype(bf16)
            if back == 0:
                ownbuf[pl.ds(piece * rows_t, rows_t)] = rows
            return carry

        lax.fori_loop(0, group // chunk, grads, 0)
        for dx in range(NX):
            dy = (NY - back) % NY
            if (dx, dy) == (0, 0):
                continue
            n = xy_steps.index((dx, dy))
            xx = along(x, dx, NX)
            copy = remote(
                sendbuf.at[pl.ds(gy * part, part), xx], recvbuf.at[x * NY + y],
                r_send.at[n], r_recv.at[n], device(xx, gy, z, core),
            )
            copy.start()
            r_copies.append((copy, dx, dy))

    def page_part(p):
        total = jnp.zeros((slab, depth), f32)
        for g in range(NY):
            tokens = gbuf[g * part : (g + 1) * part].reshape(group, depth)
            total = total + jnp.dot(coef[g, p], tokens, preferred_element_type=f32)
        return total

    def other_pages(i, carry):
        pgsend[i] = page_part(2 * (1 - core) + i)
        return carry

    lax.fori_loop(0, 2, other_pages, 0)
    swap_grads = remote(pgsend, pgrecv, core_send.at[3], core_recv.at[3], partner)
    swap_grads.start()

    total = ownbuf[:, pl.ds(x, 1)].reshape(part * NZ, depth)
    for copy, dx, dy in r_copies:
        copy.wait_recv()
        source = along(x, NX - dx, NX) * NY + along(y, NY - dy, NY)
        total = total + recvbuf[source].astype(f32).reshape(part * NZ, depth)
    zsum[...] = total
    for zz in range(NZ):
        zsend[zz] = zsum[pl.ds(zz, part, stride=NZ), :]
    q_copies = []
    for d in reversed(z_steps):
        zz = along(z, d, NZ)
        copy = remote(
            zsend.at[zz], zrecv.at[z], q_send.at[d], q_recv.at[d], device(x, y, zz, core)
        )
        copy.start()
        q_copies.append((copy, d))

    def own_page(i, carry):
        pg_tile[i] = page_part(2 * core + i)
        return carry

    lax.fori_loop(0, 2, own_page, 0)
    swap_grads.wait_recv()
    pg_tile[...] += pgrecv[...]
    outs = [pltpu.make_async_copy(pg_tile, pg_ref, local_sem.at[4])]
    outs[0].start()

    swap_loss.wait_recv()
    row = lax.broadcasted_iota(jnp.int32, (wide, 2 * lanes_q), 0)
    col = lax.broadcasted_iota(jnp.int32, (wide, 2 * lanes_q), 1)
    loss = jnp.zeros((1, 2 * lanes_q), f32)
    for c in range(2):
        spread = jnp.logical_and(col == 2 * row + c, row < lanes_q).astype(f32).astype(bf16)
        loss = loss + onehot_dot(lossbuf[c], spread)
    loss_row[...] = loss
    outs.append(pltpu.make_async_copy(loss_row, loss_ref, local_sem.at[5]))
    outs[1].start()

    total = zsend[z]
    for copy, d in q_copies:
        copy.wait_recv()
        total = total + zrecv[along(z, NZ - d, NZ)]
    qg_tile[0] = total
    outs.append(pltpu.make_async_copy(qg_tile, qg_ref, local_sem.at[6]))
    outs[2].start()

    for d in z_steps:
        z_copy(core, d).wait_send()

    @pl.when(core == 1)
    def _():
        z_copy(1, 0).wait_send()

    @pl.when(core == 0)
    def _():
        for dx, dy in xy_steps:
            g_copy(0, dx, dy).wait_send()
        for dx, dy in [(0, 0)] + xy_steps:
            g_copy(1, dx, dy).wait_send()

    for copy in l_copies + s_copies + x_copies:
        copy.wait_send()
    for copy in [swap_patches, swap_counts, swap_loss, swap_grads]:
        copy.wait_send()
    for copy, *_ in r_copies + q_copies:
        copy.wait_send()
    for copy in outs:
        copy.wait()


def hand_on(*refs):
    sources, targets, tiles, sem = refs[:3], refs[3:6], refs[6:9], refs[9]
    takes = [pltpu.make_async_copy(s, t, sem.at[i]) for i, (s, t) in enumerate(zip(sources, tiles))]
    gives = [pltpu.make_async_copy(t, o, sem.at[i]) for i, (t, o) in enumerate(zip(tiles, targets))]
    for copy in takes:
        copy.start()
    for take, give in zip(takes, gives):
        take.wait()
        give.start()
    for copy in gives:
        copy.wait()


def shards(sizes, query_tokens, page_patches, patch_counts, positive_page):
    NX, NY, NZ = sizes
    _, query_len, depth = query_tokens.shape
    slab = page_patches.shape[1]
    part = query_len // NY
    lanes_q = NX * NZ
    group = part * lanes_q
    wide = 2 * lanes_q
    peers = NX * NY - 1
    vmem = pltpu.VMEM
    dma = pltpu.SemaphoreType.DMA
    shapes = [
        jax.ShapeDtypeStruct((2, slab, depth), f32),
        jax.ShapeDtypeStruct((1, part, depth), f32),
        jax.ShapeDtypeStruct((1, 2 * lanes_q), f32),
    ]
    hbm = pl.BlockSpec(memory_space=pltpu.HBM)
    loss, query_grad, page_grad = pl.pallas_call(
        functools.partial(kernel, sizes),
        out_shape=shapes[::-1],
        in_specs=[hbm] * 4,
        out_specs=[hbm] * 3,
        scratch_shapes=[
            pltpu.SMEM((2,), jnp.int32),
            vmem((1, 2 * lanes_q), jnp.int32),
            vmem((1, 2 * lanes_q), f32),
            vmem((1, part, depth), f32),
            vmem((2, slab, depth), f32),
            vmem((2, NZ, part, depth), bf16),
            vmem((NZ * part, depth), f32),
            vmem((part, NZ, depth), bf16),
            vmem((query_len, NX, NZ, depth), bf16),
            vmem((4, slab, depth), bf16),
            vmem((4, slab, depth), bf16),
            vmem((depth, 4 * slab), bf16),
            vmem((2, 8, depth), f32),
            vmem((NY, 4, slab, group), f32),
            vmem((NY, 4, slab, group), bf16),
            vmem((NY, 4, group), f32),
            vmem((NY, NY, 4, group), f32),
            vmem((NY, 4, group), f32),
            vmem((NY, 4, group), f32),
            vmem((slab, min(lane_chunk, group)), f32),
            vmem((slab, min(lane_chunk, group)), f32),
            vmem((NZ, 2, wide), f32),
            vmem((NX, 2, wide), f32),
            vmem((2, 1, wide), f32),
            vmem((query_len, NX, NZ, depth), bf16),
            vmem((part, NX, NZ, depth), f32),
            vmem((NX * NY, part, NZ, depth), bf16),
            vmem((part * NZ, depth), f32),
            vmem((NZ, part, depth), f32),
            vmem((NZ, part, depth), f32),
            vmem((2, slab, depth), f32),
            vmem((2, slab, depth), f32),
            pltpu.SemaphoreType.REGULAR,
            dma((7,)),
            dma((4,)), dma((4,)),
            dma((NZ,)), dma((2, NZ)),
            dma((2, peers + 1)), dma((peers + 1,)),
            dma((NY, NY - 1)), dma((NY, NY - 1)),
            dma((NZ,)), dma((NZ,)),
            dma((NX,)), dma((NX,)),
            dma((peers,)), dma((peers,)),
            dma((NZ,)), dma((NZ,)),
        ],
        compiler_params=pltpu.CompilerParams(
            collective_id=0, has_side_effects=True, vmem_limit_bytes=56 * 1024 * 1024
        ),
    )(query_tokens, page_patches, patch_counts, positive_page.reshape(1, 2 * lanes_q))
    page_grad, query_grad, loss = pl.pallas_call(
        hand_on,
        out_shape=shapes,
        in_specs=[hbm] * 3,
        out_specs=[hbm] * 3,
        scratch_shapes=[vmem(shape.shape, f32) for shape in shapes] + [dma((3,))],
    )(page_grad, query_grad, loss)
    return (loss.reshape(2 * lanes_q), query_grad, page_grad)


def solution(mesh):
    chips = mesh.shape["pages"] // 2
    sizes = (chips // chips_z, mesh.shape["queries"], chips_z)
    in_specs = (P("pages", None, None), P("pages", "queries", None), P("pages"), P())
    out_specs = (P(), P("pages", "queries", None), P("pages", "queries", None))
    return jax.shard_map(
        functools.partial(shards, sizes),
        mesh=mesh, in_specs=in_specs, out_specs=out_specs, check_vma=False,
    )
```

```python
import functools
import math

import jax
import jax.numpy as jnp
from jax import lax
from jax.experimental import pallas as pl
from jax.experimental.pallas import tpu as pltpu
from jax.sharding import PartitionSpec as P

smooth_tau = 0.05
page_temp = 0.02
neg_large = -1e30
chips_z = 16
lane_chunk = 256
MESH = pl.DeviceIdType.MESH
f32, bf16 = jnp.float32, jnp.bfloat16


def ring_offsets(count):
    near = sorted(range(count), key=lambda d: (min(d, count - d), d))
    return near


def onehot_dot(value, select):
    high = value.astype(bf16).astype(f32)
    rest = value - high
    mid = rest.astype(bf16).astype(f32)
    low = rest - mid
    row = lax.broadcasted_iota(jnp.int32, (8, value.shape[1]), 0)
    stack = jnp.where(row == 0, high, jnp.where(row == 1, mid, jnp.where(row == 2, low, 0.0)))
    out = jnp.dot(stack.astype(bf16), select, preferred_element_type=f32)
    return (out[0:1] + out[1:2]) + out[2:3]


def merge_lse(rows, scale):
    top = jnp.max(rows, axis=0, keepdims=True)
    total = jnp.sum(jnp.exp((rows - top) * scale), axis=0, keepdims=True)
    return (top + jnp.log(total) / scale)[0]


def kernel(
    sizes, tok_ref, pat_ref, cnt_ref, pos_ref, loss_ref, qg_ref, pg_ref,
    counts, pos_row, loss_row, qg_tile, pg_tile,
    zbuf, zflat, stage, gbuf, pbuf, bias, ptran, cbuf, ebuf, coef, mbuf, lbuf, erbuf, rbuf,
    held_a, held_b, softz, softx, lossbuf, sendbuf, ownbuf, recvbuf, zsum, zsend, zrecv, pgsend, pgrecv,
    ready, local_sem, core_send, core_recv, z_send, z_recv, g_send, g_recv, l_send, l_recv,
    s_send, s_recv, x_send, x_recv, r_send, r_recv, q_send, q_recv,
):
    NX, NY, NZ = sizes
    lanes_q = NX * NZ
    query_len = tok_ref.shape[1]
    part = query_len // NY
    group = part * lanes_q
    slab = pat_ref.shape[1]
    held = (held_a, held_b)
    inv_tau = 1.0 / smooth_tau
    exp_scale = inv_tau * math.log2(math.e)
    chunk = min(lane_chunk, group)
    wide = 2 * lanes_q

    me = lax.axis_index("pages")
    y = lax.axis_index("queries")
    core = lax.rem(me, 2)
    chip = lax.div(me, 2)
    z = lax.rem(chip, NZ)
    x = lax.div(chip, NZ)

    def device(xx, yy, zz, cc):
        return ((xx * NZ + zz) * 2 + cc, yy)

    def along(pos, step, count):
        return lax.rem(pos + step, count)

    partner = device(x, y, z, 1 - core)
    z_steps = ring_offsets(NZ)[1:]
    y_steps = ring_offsets(NY)
    xy_steps = [(dx, dy) for dy in y_steps for dx in ring_offsets(NX) if (dx, dy) != (0, 0)]

    def remote(src, dst, ssem, rsem, target):
        return pltpu.make_async_remote_copy(
            src_ref=src, dst_ref=dst, send_sem=ssem, recv_sem=rsem,
            device_id=target, device_id_type=MESH,
        )

    barrier = pltpu.get_barrier_semaphore()

    def greet(target):
        pl.semaphore_signal(barrier, inc=1, device_id=target, device_id_type=MESH)

    @pl.when(core == 0)
    def _():
        for cc in range(2):
            for d in reversed(z_steps):
                greet(device(x, y, along(z, d, NZ), cc))
            for dx, dy in xy_steps:
                greet(device(along(x, dx, NX), along(y, dy, NY), z, cc))
        greet(partner)

    my_tokens = tok_ref.at[0, pl.ds(pl.multiple_of(y * part, part), part), :]
    own_pages = pl.ds(core * 2, 2)
    own_counts = pltpu.make_async_copy(cnt_ref, counts, local_sem.at[2])
    own_counts.start()
    own_pos = pltpu.make_async_copy(pos_ref, pos_row, local_sem.at[3])
    own_pos.start()
    own_tokens = pltpu.make_async_copy(my_tokens, zbuf.at[core, z], local_sem.at[0])
    own_tokens.start()
    own_patches = pltpu.make_async_copy(pat_ref, pbuf.at[own_pages], local_sem.at[1])
    own_patches.start()
    own_counts.wait()
    for i in range(2):
        cbuf[core, pl.ds(i, 1), :] = jnp.full((1, cbuf.shape[2]), counts[i], jnp.int32).astype(f32)

    pl.semaphore_wait(barrier, len(z_steps) + len(xy_steps) + core)

    @pl.when(core == 1)
    def _():
        for dx, dy in xy_steps:
            pl.semaphore_signal(
                ready, inc=1, device_id=device(along(x, dx, NX), along(y, dy, NY), z, 0),
                device_id_type=MESH,
            )

    def z_copy(source_core, d):
        return remote(
            my_tokens, zbuf.at[source_core, z], z_send.at[d], z_recv.at[source_core, d],
            device(x, y, along(z, d, NZ), 0),
        )

    for d in reversed(z_steps):
        z_copy(core, d).start()
    swap_patches = remote(
        pat_ref, pbuf.at[own_pages], core_send.at[0], core_recv.at[0], partner
    )
    swap_counts = remote(cbuf.at[core], cbuf.at[core], core_send.at[1], core_recv.at[1], partner)

    @pl.when(core == 1)
    def _():
        z_copy(1, 0).start()

    @pl.when(core == 0)
    def _():
        z_copy(1, 0).wait_recv()

    swap_patches.start()
    swap_counts.start()

    own_patches.wait()
    swap_counts.wait_recv()
    swap_patches.wait_recv()
    depth = pbuf.shape[2]
    slot = y * slab + lax.broadcasted_iota(jnp.int32, (slab, depth), 0)
    first_lane = lax.broadcasted_iota(jnp.int32, (slab, depth), 1) == 0
    for p in range(4):
        count = cbuf[p // 2, pl.ds(p % 2, 1), :].astype(jnp.int32)
        dead = jnp.logical_and(slot >= count, first_lane)
        bias[p] = jnp.where(dead, neg_large, 0.0).astype(bf16)
        ptran[:, p * slab : (p + 1) * slab] = pbuf[p].astype(f32).T.astype(bf16)
    select = (
        lax.broadcasted_iota(jnp.int32, (2 * lanes_q, wide), 0)
        == 2 * lax.rem(lax.broadcasted_iota(jnp.int32, (2 * lanes_q, wide), 1), lanes_q) + core
    )
    own_pos.wait()
    positive = jnp.dot(
        jnp.broadcast_to(pos_row[...].astype(f32), (8, 2 * lanes_q)).astype(bf16),
        select.astype(bf16), preferred_element_type=f32,
    )[0:1]
    log_count = smooth_tau * jnp.log(
        jnp.concatenate([cbuf[0, 0:2, 0:wide], cbuf[1, 0:2, 0:wide]], axis=0)
    )

    own_tokens.wait()
    mine = gbuf.at[pl.ds(y * part, part), x]

    def g_copy(dx, dy):
        return remote(
            mine, mine, g_send.at[dy * NX + dx], g_recv.at[dy * NX + dx],
            device(along(x, dx, NX), along(y, dy, NY), z, core),
        )

    hand_tokens = remote(stage, mine, g_send.at[0], g_recv.at[0], partner)

    @pl.when(core == 0)
    def _():
        for d in z_steps:
            z_copy(0, d).wait_recv()
        zflat[...] = zbuf[0].astype(f32).reshape(zflat.shape)
        for t in range(part):
            gbuf[y * part + t, x] = zflat[pl.ds(t, NZ, stride=part), :].astype(bf16)
        for dx, dy in xy_steps:
            g_copy(dx, dy).start()
        for d in z_steps:
            z_copy(1, d).wait_recv()
        zflat[...] = zbuf[1].astype(f32).reshape(zflat.shape)
        for t in range(part):
            stage[t] = zflat[pl.ds(t, NZ, stride=part), :].astype(bf16)
        pl.semaphore_wait(ready, len(xy_steps))
        hand_tokens.start()

    @pl.when(core == 1)
    def _():
        hand_tokens.wait_recv()
        for dx, dy in xy_steps:
            g_copy(dx, dy).start()

    ones = jnp.where(lax.broadcasted_iota(jnp.int32, (chunk, depth), 1) == 0, 1.0, 0.0).astype(bf16)
    rows_t = chunk // lanes_q
    l_copies = []
    for k, back in enumerate(y_steps):
        for dx in range(NX):
            if (dx, back) != (0, 0):
                g_copy(dx, back).wait_recv()
        gy = along(y, NY - back, NY)

        def scores(block):
            p, piece = block % 4, block // 4
            tokens = gbuf[pl.ds(gy * part + piece * rows_t, rows_t)].reshape(chunk, depth)
            similar = lax.dot_general(
                jnp.concatenate([pbuf[p], bias[p]], axis=1),
                jnp.concatenate([tokens, ones], axis=1),
                (((1,), (1,)), ((), ())), preferred_element_type=f32,
            )
            held[block % 2][...] = similar
            return jnp.max(similar, axis=0, keepdims=True)

        def exponents(block, top):
            p, piece = block % 4, block // 4
            lanes = slice(piece * chunk, (piece + 1) * chunk)
            terms = jnp.exp2((held[block % 2][...] - top) * exp_scale)
            ebuf[gy, p, :, lanes] = terms
            total = jnp.sum(terms, axis=0, keepdims=True)
            mbuf[gy, p : p + 1, lanes] = top
            lbuf[y, gy, p : p + 1, lanes] = top + smooth_tau * jnp.log(total)

        blocks = 4 * (group // chunk)
        top = scores(0)
        for block in range(blocks):
            following = scores(block + 1) if block + 1 < blocks else None
            exponents(block, top)
            top = following
        for n, dy in enumerate(y_steps[1:]):
            copy = remote(
                lbuf.at[y, gy], lbuf.at[y, gy], l_send.at[k, n], l_recv.at[k, n],
                device(x, along(y, dy, NY), z, core),
            )
            copy.start()
            l_copies.append(copy)

    for copy in l_copies:
        copy.wait_recv()
    sums = jnp.zeros((4, wide), f32)
    for g in range(NY):
        lse = merge_lse(lbuf[:, g], inv_tau)
        erbuf[g] = jnp.exp((mbuf[g] - lse) * inv_tau)
        for i in range(group // wide):
            sums = sums + lse[:, i * wide : (i + 1) * wide]
    sums = sums + pltpu.roll(sums, lanes_q, 1)
    logits = (sums - query_len * log_count) / page_temp
    page_id = (chip * 4 + lax.broadcasted_iota(jnp.int32, (4, wide), 0)).astype(f32)
    is_positive = page_id == positive

    softz[z, 0:1, :] = merge_lse(logits[:, None, :], 1.0)
    softz[z, 1:2, :] = jnp.sum(jnp.where(is_positive, logits, 0.0), axis=0, keepdims=True)
    s_copies = []
    for d in reversed(z_steps):
        copy = remote(
            softz.at[z], softz.at[z], s_send.at[d], s_recv.at[d],
            device(x, y, along(z, d, NZ), core),
        )
        copy.start()
        s_copies.append(copy)
    for copy in s_copies:
        copy.wait_recv()
    softx[x, 0:1, :] = merge_lse(softz[:, 0:1, :], 1.0)
    softx[x, 1:2, :] = jnp.sum(softz[:, 1:2, :], axis=0)
    x_copies = []
    for d in ring_offsets(NX)[1:]:
        copy = remote(
            softx.at[x], softx.at[x], x_send.at[d], x_recv.at[d],
            device(along(x, d, NX), y, z, core),
        )
        copy.start()
        x_copies.append(copy)
    for copy in x_copies:
        copy.wait_recv()
    all_lse = merge_lse(softx[:, 0:1, :], 1.0)
    lossbuf[core] = all_lse - jnp.sum(softx[:, 1:2, :], axis=0)
    swap_loss = remote(lossbuf.at[core], lossbuf.at[core], core_send.at[2], core_recv.at[2], partner)
    swap_loss.start()
    weights = (jnp.exp(logits - all_lse) - is_positive.astype(f32)) / page_temp
    wide_weights = jnp.concatenate([weights] * (group // wide), axis=1)
    for g in range(NY):
        rbuf[g] = erbuf[g] * wide_weights

    r_copies = []
    for back in reversed(y_steps):
        gy = along(y, NY - back, NY)

        def backward(p, carry):
            coef[gy, p] = (ebuf[gy, p] * rbuf[gy, pl.ds(p, 1), :]).astype(bf16)
            return carry

        lax.fori_loop(0, 4, backward, 0)

        def grads(piece, carry):
            lanes = pl.ds(pl.multiple_of(piece * chunk, chunk), chunk)
            across = jnp.dot(
                ptran[...], coef[gy, :, :, lanes].reshape(4 * slab, chunk),
                preferred_element_type=f32,
            )
            rows = across.T.reshape(rows_t, NX, NZ, depth)
            sendbuf[pl.ds(gy * part + piece * rows_t, rows_t)] = rows.astype(bf16)
            if back == 0:
                ownbuf[pl.ds(piece * rows_t, rows_t)] = rows
            return carry

        lax.fori_loop(0, group // chunk, grads, 0)
        for dx in range(NX):
            dy = (NY - back) % NY
            if (dx, dy) == (0, 0):
                continue
            n = xy_steps.index((dx, dy))
            xx = along(x, dx, NX)
            copy = remote(
                sendbuf.at[pl.ds(gy * part, part), xx], recvbuf.at[x * NY + y],
                r_send.at[n], r_recv.at[n], device(xx, gy, z, core),
            )
            copy.start()
            r_copies.append((copy, dx, dy))

    def page_part(p):
        total = jnp.zeros((slab, depth), f32)
        for g in range(NY):
            tokens = gbuf[g * part : (g + 1) * part].reshape(group, depth)
            total = total + jnp.dot(coef[g, p], tokens, preferred_element_type=f32)
        return total

    def other_pages(i, carry):
        pgsend[i] = page_part(2 * (1 - core) + i)
        return carry

    lax.fori_loop(0, 2, other_pages, 0)
    swap_grads = remote(pgsend, pgrecv, core_send.at[3], core_recv.at[3], partner)
    swap_grads.start()

    total = ownbuf[:, pl.ds(x, 1)].reshape(part * NZ, depth)
    for copy, dx, dy in r_copies:
        copy.wait_recv()
        source = along(x, NX - dx, NX) * NY + along(y, NY - dy, NY)
        total = total + recvbuf[source].astype(f32).reshape(part * NZ, depth)
    zsum[...] = total
    for zz in range(NZ):
        zsend[zz] = zsum[pl.ds(zz, part, stride=NZ), :]
    q_copies = []
    for d in reversed(z_steps):
        zz = along(z, d, NZ)
        copy = remote(
            zsend.at[zz], zrecv.at[z], q_send.at[d], q_recv.at[d], device(x, y, zz, core)
        )
        copy.start()
        q_copies.append((copy, d))

    def own_page(i, carry):
        pg_tile[i] = page_part(2 * core + i)
        return carry

    lax.fori_loop(0, 2, own_page, 0)
    swap_grads.wait_recv()
    pg_tile[...] += pgrecv[...]
    outs = [pltpu.make_async_copy(pg_tile, pg_ref, local_sem.at[4])]
    outs[0].start()

    swap_loss.wait_recv()
    row = lax.broadcasted_iota(jnp.int32, (wide, 2 * lanes_q), 0)
    col = lax.broadcasted_iota(jnp.int32, (wide, 2 * lanes_q), 1)
    loss = jnp.zeros((1, 2 * lanes_q), f32)
    for c in range(2):
        spread = jnp.logical_and(col == 2 * row + c, row < lanes_q).astype(f32).astype(bf16)
        loss = loss + onehot_dot(lossbuf[c], spread)
    loss_row[...] = loss
    outs.append(pltpu.make_async_copy(loss_row, loss_ref, local_sem.at[5]))
    outs[1].start()

    total = zsend[z]
    for copy, d in q_copies:
        copy.wait_recv()
        total = total + zrecv[along(z, NZ - d, NZ)]
    qg_tile[0] = total
    outs.append(pltpu.make_async_copy(qg_tile, qg_ref, local_sem.at[6]))
    outs[2].start()

    for d in z_steps:
        z_copy(core, d).wait_send()

    @pl.when(core == 1)
    def _():
        z_copy(1, 0).wait_send()

    @pl.when(core == 0)
    def _():
        hand_tokens.wait_send()

    for dx, dy in xy_steps:
        g_copy(dx, dy).wait_send()
    for copy in l_copies + s_copies + x_copies:
        copy.wait_send()
    for copy in [swap_patches, swap_counts, swap_loss, swap_grads]:
        copy.wait_send()
    for copy, *_ in r_copies + q_copies:
        copy.wait_send()
    for copy in outs:
        copy.wait()


def hand_on(*refs):
    sources, targets, tiles, sem = refs[:3], refs[3:6], refs[6:9], refs[9]
    rows = sources[0].shape[1] // 2
    parts = [(0, (i, pl.ds(j * rows, rows))) for i in range(2) for j in range(2)] + [(1, ()), (2, ())]
    takes, gives = [], []
    for n, (i, where) in enumerate(parts):
        source, tile, target = (r[i].at[where] if where else r[i] for r in (sources, tiles, targets))
        takes.append(pltpu.make_async_copy(source, tile, sem.at[0, n]))
        gives.append(pltpu.make_async_copy(tile, target, sem.at[1, n]))
    for copy in takes:
        copy.start()
    for take, give in zip(takes, gives):
        take.wait()
        give.start()
    for copy in gives:
        copy.wait()


def shards(sizes, query_tokens, page_patches, patch_counts, positive_page):
    NX, NY, NZ = sizes
    _, query_len, depth = query_tokens.shape
    slab = page_patches.shape[1]
    part = query_len // NY
    lanes_q = NX * NZ
    group = part * lanes_q
    wide = 2 * lanes_q
    peers = NX * NY - 1
    vmem = pltpu.VMEM
    dma = pltpu.SemaphoreType.DMA
    shapes = [
        jax.ShapeDtypeStruct((2, slab, depth), f32),
        jax.ShapeDtypeStruct((1, part, depth), f32),
        jax.ShapeDtypeStruct((1, 2 * lanes_q), f32),
    ]
    hbm = pl.BlockSpec(memory_space=pltpu.HBM)
    loss, query_grad, page_grad = pl.pallas_call(
        functools.partial(kernel, sizes),
        out_shape=shapes[::-1],
        in_specs=[hbm] * 4,
        out_specs=[hbm] * 3,
        scratch_shapes=[
            pltpu.SMEM((2,), jnp.int32),
            vmem((1, 2 * lanes_q), jnp.int32),
            vmem((1, 2 * lanes_q), f32),
            vmem((1, part, depth), f32),
            vmem((2, slab, depth), f32),
            vmem((2, NZ, part, depth), bf16),
            vmem((NZ * part, depth), f32),
            vmem((part, NZ, depth), bf16),
            vmem((query_len, NX, NZ, depth), bf16),
            vmem((4, slab, depth), bf16),
            vmem((4, slab, depth), bf16),
            vmem((depth, 4 * slab), bf16),
            vmem((2, 8, depth), f32),
            vmem((NY, 4, slab, group), f32),
            vmem((NY, 4, slab, group), bf16),
            vmem((NY, 4, group), f32),
            vmem((NY, NY, 4, group), f32),
            vmem((NY, 4, group), f32),
            vmem((NY, 4, group), f32),
            vmem((slab, min(lane_chunk, group)), f32),
            vmem((slab, min(lane_chunk, group)), f32),
            vmem((NZ, 2, wide), f32),
            vmem((NX, 2, wide), f32),
            vmem((2, 1, wide), f32),
            vmem((query_len, NX, NZ, depth), bf16),
            vmem((part, NX, NZ, depth), f32),
            vmem((NX * NY, part, NZ, depth), bf16),
            vmem((part * NZ, depth), f32),
            vmem((NZ, part, depth), f32),
            vmem((NZ, part, depth), f32),
            vmem((2, slab, depth), f32),
            vmem((2, slab, depth), f32),
            pltpu.SemaphoreType.REGULAR,
            dma((7,)),
            dma((4,)), dma((4,)),
            dma((NZ,)), dma((2, NZ)),
            dma((peers + 1,)), dma((peers + 1,)),
            dma((NY, NY - 1)), dma((NY, NY - 1)),
            dma((NZ,)), dma((NZ,)),
            dma((NX,)), dma((NX,)),
            dma((peers,)), dma((peers,)),
            dma((NZ,)), dma((NZ,)),
        ],
        compiler_params=pltpu.CompilerParams(
            collective_id=0, has_side_effects=True, vmem_limit_bytes=56 * 1024 * 1024
        ),
    )(query_tokens, page_patches, patch_counts, positive_page.reshape(1, 2 * lanes_q))
    page_grad, query_grad, loss = pl.pallas_call(
        hand_on,
        out_shape=shapes,
        in_specs=[hbm] * 3,
        out_specs=[hbm] * 3,
        scratch_shapes=[vmem(shape.shape, f32) for shape in shapes] + [dma((2, 6))],
    )(page_grad, query_grad, loss)
    return (loss.reshape(2 * lanes_q), query_grad, page_grad)


def solution(mesh):
    chips = mesh.shape["pages"] // 2
    sizes = (chips // chips_z, mesh.shape["queries"], chips_z)
    in_specs = (P("pages", None, None), P("pages", "queries", None), P("pages"), P())
    out_specs = (P(), P("pages", "queries", None), P("pages", "queries", None))
    return jax.shard_map(
        functools.partial(shards, sizes),
        mesh=mesh, in_specs=in_specs, out_specs=out_specs, check_vma=False,
    )
```

```python
import functools
import math

import jax
import jax.numpy as jnp
from jax import lax
from jax.experimental import pallas as pl
from jax.experimental.pallas import tpu as pltpu
from jax.sharding import PartitionSpec as P

smooth_tau = 0.05
page_temp = 0.02
neg_large = -1e30
chips_z = 16
lane_chunk = 256
MESH = pl.DeviceIdType.MESH
f32, bf16 = jnp.float32, jnp.bfloat16


def ring_offsets(count):
    near = sorted(range(count), key=lambda d: (min(d, count - d), d))
    return near


def onehot_dot(value, select):
    high = value.astype(bf16).astype(f32)
    rest = value - high
    mid = rest.astype(bf16).astype(f32)
    low = rest - mid
    row = lax.broadcasted_iota(jnp.int32, (8, value.shape[1]), 0)
    stack = jnp.where(row == 0, high, jnp.where(row == 1, mid, jnp.where(row == 2, low, 0.0)))
    out = jnp.dot(stack.astype(bf16), select, preferred_element_type=f32)
    return (out[0:1] + out[1:2]) + out[2:3]


def merge_lse(rows, scale):
    top = jnp.max(rows, axis=0, keepdims=True)
    total = jnp.sum(jnp.exp((rows - top) * scale), axis=0, keepdims=True)
    return (top + jnp.log(total) / scale)[0]


def kernel(
    sizes, tok_ref, pat_ref, cnt_ref, pos_ref, loss_ref, qg_ref, pg_ref,
    counts, pos_row,
    zbuf, zflat, gbuf, pbuf, bias, ptran, cbuf, ebuf, coef, mbuf, lbuf, erbuf, rbuf,
    held_a, held_b, softs, lossbuf, sendbuf, ownbuf, recvbuf, zsum, zsend, zrecv, pgsend, pgrecv,
    local_sem, core_send, core_recv, z_send, z_recv, g_send, g_recv, l_send, l_recv,
    s_send, s_recv, r_send, r_recv, q_send, q_recv,
):
    NX, NY, NZ = sizes
    lanes_q = NX * NZ
    query_len = tok_ref.shape[1]
    part = query_len // NY
    group = part * lanes_q
    slab = pat_ref.shape[1]
    held = (held_a, held_b)
    inv_tau = 1.0 / smooth_tau
    exp_scale = inv_tau * math.log2(math.e)
    chunk = min(lane_chunk, group)
    wide = 2 * lanes_q

    me = lax.axis_index("pages")
    y = lax.axis_index("queries")
    core = lax.rem(me, 2)
    chip = lax.div(me, 2)
    z = lax.rem(chip, NZ)
    x = lax.div(chip, NZ)

    def device(xx, yy, zz, cc):
        return ((xx * NZ + zz) * 2 + cc, yy)

    def along(pos, step, count):
        return lax.rem(pos + step, count)

    partner = device(x, y, z, 1 - core)
    z_steps = ring_offsets(NZ)[1:]
    y_steps = ring_offsets(NY)
    xy_steps = [(dx, dy) for dy in y_steps for dx in ring_offsets(NX) if (dx, dy) != (0, 0)]

    def remote(src, dst, ssem, rsem, target):
        return pltpu.make_async_remote_copy(
            src_ref=src, dst_ref=dst, send_sem=ssem, recv_sem=rsem,
            device_id=target, device_id_type=MESH,
        )

    barrier = pltpu.get_barrier_semaphore()

    def greet(target):
        pl.semaphore_signal(barrier, inc=1, device_id=target, device_id_type=MESH)

    for d in reversed(z_steps):
        greet(device(x, y, along(z, d, NZ), core))
    for dx, dy in xy_steps:
        greet(device(along(x, dx, NX), along(y, dy, NY), z, core))
    greet(partner)

    my_tokens = tok_ref.at[0, pl.ds(pl.multiple_of(y * part, part), part), :]
    own_pages = pl.ds(core * 2, 2)
    own_counts = pltpu.make_async_copy(cnt_ref, counts, local_sem.at[2])
    own_counts.start()
    own_pos = pltpu.make_async_copy(pos_ref, pos_row, local_sem.at[3])
    own_pos.start()
    own_tokens = pltpu.make_async_copy(my_tokens, zbuf.at[z], local_sem.at[0])
    own_tokens.start()
    own_patches = pltpu.make_async_copy(pat_ref, pbuf.at[own_pages], local_sem.at[1])
    own_patches.start()
    own_counts.wait()
    for i in range(2):
        cbuf[core, pl.ds(i, 1), :] = jnp.full((1, cbuf.shape[2]), counts[i], jnp.int32).astype(f32)

    pl.semaphore_wait(barrier, len(z_steps) + len(xy_steps) + 1)

    z_copies = []
    for d in reversed(z_steps):
        copy = remote(
            my_tokens, zbuf.at[z], z_send.at[d], z_recv.at[d], device(x, y, along(z, d, NZ), core)
        )
        copy.start()
        z_copies.append(copy)
    swap_patches = remote(
        pat_ref, pbuf.at[own_pages], core_send.at[0], core_recv.at[0], partner
    )
    swap_patches.start()
    swap_counts = remote(cbuf.at[core], cbuf.at[core], core_send.at[1], core_recv.at[1], partner)
    swap_counts.start()

    own_patches.wait()
    swap_counts.wait_recv()
    swap_patches.wait_recv()
    depth = pbuf.shape[2]
    slot = y * slab + lax.broadcasted_iota(jnp.int32, (slab, depth), 0)
    first_lane = lax.broadcasted_iota(jnp.int32, (slab, depth), 1) == 0
    for p in range(4):
        count = cbuf[p // 2, pl.ds(p % 2, 1), :].astype(jnp.int32)
        dead = jnp.logical_and(slot >= count, first_lane)
        bias[p] = jnp.where(dead, neg_large, 0.0).astype(bf16)
        ptran[:, p * slab : (p + 1) * slab] = pbuf[p].astype(f32).T.astype(bf16)
    select = (
        lax.broadcasted_iota(jnp.int32, (2 * lanes_q, wide), 0)
        == 2 * lax.rem(lax.broadcasted_iota(jnp.int32, (2 * lanes_q, wide), 1), lanes_q) + core
    )
    own_pos.wait()
    positive = jnp.dot(
        jnp.broadcast_to(pos_row[...].astype(f32), (8, 2 * lanes_q)).astype(bf16),
        select.astype(bf16), preferred_element_type=f32,
    )[0:1]
    log_count = smooth_tau * jnp.log(
        jnp.concatenate([cbuf[0, 0:2, 0:wide], cbuf[1, 0:2, 0:wide]], axis=0)
    )

    own_tokens.wait()
    for copy in z_copies:
        copy.wait_recv()
    zflat[...] = zbuf[...].astype(f32).reshape(zflat.shape)
    for t in range(part):
        gbuf[y * part + t, x] = zflat[pl.ds(t, NZ, stride=part), :].astype(bf16)

    pieces = group // chunk
    rows_t = chunk // lanes_q
    g_copies = {}
    for dx, dy in xy_steps:
        count = pieces if dy == y_steps[-1] else 1
        for h in range(count):
            n = (h * NY + dy) * NX + dx
            mine = gbuf.at[pl.ds(y * part + h * (part // count), part // count), x]
            g_copies[dx, dy, h] = remote(
                mine, mine, g_send.at[n], g_recv.at[n],
                device(along(x, dx, NX), along(y, dy, NY), z, core),
            )
    for (dx, dy, h), copy in sorted(
        g_copies.items(), key=lambda item: (y_steps.index(item[0][1]), item[0][2])
    ):
        copy.start()

    ones = jnp.where(lax.broadcasted_iota(jnp.int32, (chunk, depth), 1) == 0, 1.0, 0.0).astype(bf16)
    l_copies = []
    for k, back in enumerate(y_steps):
        def arrive(h):
            for dx in range(NX):
                if (dx, back, h) in g_copies:
                    g_copies[dx, back, h].wait_recv()

        arrive(0)
        gy = along(y, NY - back, NY)

        def scores(block):
            p, piece = block % 4, block // 4
            tokens = gbuf[pl.ds(gy * part + piece * rows_t, rows_t)].reshape(chunk, depth)
            similar = lax.dot_general(
                jnp.concatenate([pbuf[p], bias[p]], axis=1),
                jnp.concatenate([tokens, ones], axis=1),
                (((1,), (1,)), ((), ())), preferred_element_type=f32,
            )
            held[block % 2][...] = similar
            return jnp.max(similar, axis=0, keepdims=True)

        def exponents(block, top):
            p, piece = block % 4, block // 4
            lanes = slice(piece * chunk, (piece + 1) * chunk)
            terms = jnp.exp2((held[block % 2][...] - top) * exp_scale)
            ebuf[gy, p, :, lanes] = terms
            total = jnp.sum(terms, axis=0, keepdims=True)
            mbuf[gy, p : p + 1, lanes] = top
            lbuf[y, gy, p : p + 1, lanes] = top + smooth_tau * jnp.log(total)

        blocks = 4 * (group // chunk)
        top = scores(0)
        for block in range(blocks):
            after = block + 1
            late = after < blocks and after % 4 == 0 and back == y_steps[-1]
            if late:
                exponents(block, top)
                arrive(after // 4)
            following = scores(after) if after < blocks else None
            if not late:
                exponents(block, top)
            top = following
        for n, dy in enumerate(y_steps[1:]):
            copy = remote(
                lbuf.at[y, gy], lbuf.at[y, gy], l_send.at[k, n], l_recv.at[k, n],
                device(x, along(y, dy, NY), z, core),
            )
            copy.start()
            l_copies.append(copy)

    for copy in l_copies:
        copy.wait_recv()
    sums = jnp.zeros((4, wide), f32)
    for g in range(NY):
        lse = merge_lse(lbuf[:, g], inv_tau)
        erbuf[g] = jnp.exp((mbuf[g] - lse) * inv_tau)
        for i in range(group // wide):
            sums = sums + lse[:, i * wide : (i + 1) * wide]
    sums = sums + pltpu.roll(sums, lanes_q, 1)
    logits = (sums - query_len * log_count) / page_temp
    page_id = (chip * 4 + lax.broadcasted_iota(jnp.int32, (4, wide), 0)).astype(f32)
    is_positive = page_id == positive

    low = lax.broadcasted_iota(jnp.int32, (1, wide), 1) < lanes_q
    here = x * NZ + z
    softs[here] = jnp.where(
        low, merge_lse(logits[:, None, :], 1.0),
        jnp.sum(jnp.where(is_positive, logits, 0.0), axis=0, keepdims=True),
    )
    s_copies = []
    for d in reversed(ring_offsets(NZ)):
        for dx in reversed(ring_offsets(NX)):
            if (dx, d) == (0, 0):
                continue
            copy = remote(
                softs.at[here], softs.at[here], s_send.at[dx, d], s_recv.at[dx, d],
                device(along(x, dx, NX), y, along(z, d, NZ), core),
            )
            copy.start()
            s_copies.append(copy)
    for copy in s_copies:
        copy.wait_recv()
    everyone = softs[...]
    all_lse = merge_lse(everyone, 1.0)
    all_lse = jnp.where(low, all_lse, pltpu.roll(all_lse, lanes_q, 1))
    all_pos = jnp.sum(everyone, axis=0)
    lossbuf[core] = all_lse - pltpu.roll(all_pos, lanes_q, 1)
    swap_loss = remote(lossbuf.at[core], lossbuf.at[core], core_send.at[2], core_recv.at[2], partner)
    swap_loss.start()
    weights = (jnp.exp(logits - all_lse) - is_positive.astype(f32)) / page_temp
    wide_weights = jnp.concatenate([weights] * (group // wide), axis=1)
    for g in range(NY):
        rbuf[g] = erbuf[g] * wide_weights

    r_copies = []
    for back in reversed(y_steps):
        gy = along(y, NY - back, NY)

        for piece in range(pieces):
            lanes = slice(piece * chunk, (piece + 1) * chunk)

            def backward(p, carry):
                coef[gy, p, :, lanes] = (
                    ebuf[gy, p, :, lanes] * rbuf[gy, pl.ds(p, 1), lanes]
                ).astype(bf16)
                return carry

            lax.fori_loop(0, 4, backward, 0)
            across = jnp.dot(
                ptran[...], coef[gy, :, :, lanes].reshape(4 * slab, chunk),
                preferred_element_type=f32,
            )
            rows = across.T.reshape(rows_t, NX, NZ, depth)
            sendbuf[pl.ds(gy * part + piece * rows_t, rows_t)] = rows.astype(bf16)
            if back == 0:
                ownbuf[pl.ds(piece * rows_t, rows_t)] = rows
            dy = (NY - back) % NY
            for dx in reversed(ring_offsets(NX)):
                if (dx, dy) == (0, 0):
                    continue
                n = (piece * NY + dy) * NX + dx
                xx = along(x, dx, NX)
                copy = remote(
                    sendbuf.at[pl.ds(gy * part + piece * rows_t, rows_t), xx],
                    recvbuf.at[x * NY + y, pl.ds(piece * rows_t, rows_t)],
                    r_send.at[n], r_recv.at[n], device(xx, gy, z, core),
                )
                copy.start()
                r_copies.append((copy, dx, dy, piece))

    def page_part(p):
        total = jnp.zeros((slab, depth), f32)
        for g in range(NY):
            tokens = gbuf[g * part : (g + 1) * part].reshape(group, depth)
            total = total + jnp.dot(coef[g, p], tokens, preferred_element_type=f32)
        return total

    def other_pages(i, carry):
        pgsend[i] = page_part(2 * (1 - core) + i)
        return carry

    lax.fori_loop(0, 2, other_pages, 0)
    swap_grads = remote(pgsend, pgrecv, core_send.at[3], core_recv.at[3], partner)
    swap_grads.start()

    total = ownbuf[:, pl.ds(x, 1)].reshape(part * NZ, depth)
    for copy, dx, dy, piece in sorted(r_copies, key=lambda item: item[3]):
        copy.wait_recv()
        if piece + 1 < pieces:
            continue
        source = along(x, NX - dx, NX) * NY + along(y, NY - dy, NY)
        total = total + recvbuf[source].astype(f32).reshape(part * NZ, depth)
    zsum[...] = total
    for zz in range(NZ):
        zsend[zz] = zsum[pl.ds(zz, part, stride=NZ), :]
    q_copies = []
    for d in reversed(z_steps):
        zz = along(z, d, NZ)
        copy = remote(
            zsend.at[zz], zrecv.at[z], q_send.at[d], q_recv.at[d], device(x, y, zz, core)
        )
        copy.start()
        q_copies.append((copy, d))

    def own_page(i, carry):
        pg_ref[i] = page_part(2 * core + i)
        return carry

    lax.fori_loop(0, 2, own_page, 0)
    swap_grads.wait_recv()
    pg_ref[...] += pgrecv[...]

    swap_loss.wait_recv()
    row = lax.broadcasted_iota(jnp.int32, (wide, 2 * lanes_q), 0)
    col = lax.broadcasted_iota(jnp.int32, (wide, 2 * lanes_q), 1)
    loss = jnp.zeros((1, 2 * lanes_q), f32)
    for c in range(2):
        spread = jnp.logical_and(col == 2 * row + c, row < lanes_q).astype(f32).astype(bf16)
        loss = loss + onehot_dot(lossbuf[c], spread)
    loss_ref[...] = loss

    total = zsend[z]
    for copy, d in q_copies:
        copy.wait_recv()
        total = total + zrecv[along(z, NZ - d, NZ)]
    qg_ref[0] = total

    for copy in z_copies + list(g_copies.values()) + l_copies + s_copies:
        copy.wait_send()
    for copy in [swap_patches, swap_counts, swap_loss, swap_grads]:
        copy.wait_send()
    for copy, *_ in r_copies + q_copies:
        copy.wait_send()


def hand_on(*refs):
    sources, targets, sem = refs[:3], refs[3:6], refs[6]
    copies = [pltpu.make_async_copy(s, t, sem.at[i]) for i, (s, t) in enumerate(zip(sources, targets))]
    for copy in copies:
        copy.start()
    for copy in copies:
        copy.wait()


def shards(sizes, query_tokens, page_patches, patch_counts, positive_page):
    NX, NY, NZ = sizes
    _, query_len, depth = query_tokens.shape
    slab = page_patches.shape[1]
    part = query_len // NY
    lanes_q = NX * NZ
    group = part * lanes_q
    wide = 2 * lanes_q
    pieces = group // min(lane_chunk, group)
    vmem = pltpu.VMEM
    dma = pltpu.SemaphoreType.DMA
    shapes = [
        jax.ShapeDtypeStruct((2, slab, depth), f32),
        jax.ShapeDtypeStruct((1, part, depth), f32),
        jax.ShapeDtypeStruct((1, 2 * lanes_q), f32),
    ]
    hbm = pl.BlockSpec(memory_space=pltpu.HBM)
    loss, query_grad, page_grad = pl.pallas_call(
        functools.partial(kernel, sizes),
        out_shape=[vmem(shape.shape, f32) for shape in shapes[::-1]],
        in_specs=[hbm] * 4,
        out_specs=[pl.BlockSpec(memory_space=pltpu.VMEM)] * 3,
        scratch_shapes=[
            pltpu.SMEM((2,), jnp.int32),
            vmem((1, 2 * lanes_q), jnp.int32),
            vmem((NZ, part, depth), bf16),
            vmem((NZ * part, depth), f32),
            vmem((query_len, NX, NZ, depth), bf16),
            vmem((4, slab, depth), bf16),
            vmem((4, slab, depth), bf16),
            vmem((depth, 4 * slab), bf16),
            vmem((2, 8, depth), f32),
            vmem((NY, 4, slab, group), f32),
            vmem((NY, 4, slab, group), bf16),
            vmem((NY, 4, group), f32),
            vmem((NY, NY, 4, group), f32),
            vmem((NY, 4, group), f32),
            vmem((NY, 4, group), f32),
            vmem((slab, min(lane_chunk, group)), f32),
            vmem((slab, min(lane_chunk, group)), f32),
            vmem((NX * NZ, 1, wide), f32),
            vmem((2, 1, wide), f32),
            vmem((query_len, NX, NZ, depth), bf16),
            vmem((part, NX, NZ, depth), f32),
            vmem((NX * NY, part, NZ, depth), bf16),
            vmem((part * NZ, depth), f32),
            vmem((NZ, part, depth), f32),
            vmem((NZ, part, depth), f32),
            vmem((2, slab, depth), f32),
            vmem((2, slab, depth), f32),
            dma((4,)),
            dma((4,)), dma((4,)),
            dma((NZ,)), dma((NZ,)),
            dma((pieces * NX * NY,)), dma((pieces * NX * NY,)),
            dma((NY, NY - 1)), dma((NY, NY - 1)),
            dma((NX, NZ)), dma((NX, NZ)),
            dma((pieces * NX * NY,)), dma((pieces * NX * NY,)),
            dma((NZ,)), dma((NZ,)),
        ],
        compiler_params=pltpu.CompilerParams(
            collective_id=0, has_side_effects=True, vmem_limit_bytes=56 * 1024 * 1024
        ),
    )(query_tokens, page_patches, patch_counts, positive_page.reshape(1, 2 * lanes_q))
    page_grad, query_grad, loss = pl.pallas_call(
        hand_on,
        out_shape=shapes,
        in_specs=[pl.BlockSpec(memory_space=pltpu.VMEM)] * 3,
        out_specs=[hbm] * 3,
        scratch_shapes=[dma((3,))],
    )(*(pltpu.with_memory_space_constraint(a, pltpu.VMEM) for a in (page_grad, query_grad, loss)))
    return (loss.reshape(2 * lanes_q), query_grad, page_grad)


def solution(mesh):
    chips = mesh.shape["pages"] // 2
    sizes = (chips // chips_z, mesh.shape["queries"], chips_z)
    in_specs = (P("pages", None, None), P("pages", "queries", None), P("pages"), P())
    out_specs = (P(), P("pages", "queries", None), P("pages", "queries", None))
    return jax.shard_map(
        functools.partial(shards, sizes),
        mesh=mesh, in_specs=in_specs, out_specs=out_specs, check_vma=False,
    )
```

```python
import functools
import math

import jax
import jax.numpy as jnp
from jax import lax
from jax.experimental import pallas as pl
from jax.experimental.pallas import tpu as pltpu
from jax.sharding import PartitionSpec as P

smooth_tau = 0.05
page_temp = 0.02
neg_large = -1e30
chips_z = 16
lane_chunk = 512
MESH = pl.DeviceIdType.MESH
f32, bf16 = jnp.float32, jnp.bfloat16


def ring_offsets(count):
    near = sorted(range(count), key=lambda d: (min(d, count - d), d))
    return near


def onehot_dot(value, select):
    high = value.astype(bf16).astype(f32)
    rest = value - high
    mid = rest.astype(bf16).astype(f32)
    low = rest - mid
    row = lax.broadcasted_iota(jnp.int32, (8, value.shape[1]), 0)
    stack = jnp.where(row == 0, high, jnp.where(row == 1, mid, jnp.where(row == 2, low, 0.0)))
    out = jnp.dot(stack.astype(bf16), select, preferred_element_type=f32)
    return (out[0:1] + out[1:2]) + out[2:3]


def merge_lse(rows, scale):
    top = jnp.max(rows, axis=0, keepdims=True)
    total = jnp.sum(jnp.exp((rows - top) * scale), axis=0, keepdims=True)
    return (top + jnp.log(total) / scale)[0]


def kernel(
    sizes, tok_ref, pat_ref, cnt_ref, pos_ref, loss_ref, qg_ref, pg_ref,
    counts, pos_row,
    zbuf, zflat, gbuf, pbuf, bias, ptran, cbuf, ebuf, coef, mbuf, lbuf, erbuf, rbuf,
    held_a, held_b, softs, lossbuf, sendbuf, ownbuf, recvbuf, zsum, zsend, zrecv, pgsend, pgrecv,
    local_sem, core_send, core_recv, z_send, z_recv, g_send, g_recv, l_send, l_recv,
    s_send, s_recv, r_send, r_recv, q_send, q_recv,
):
    NX, NY, NZ = sizes
    lanes_q = NX * NZ
    query_len = tok_ref.shape[1]
    part = query_len // NY
    group = part * lanes_q
    slab = pat_ref.shape[1]
    held = (held_a, held_b)
    inv_tau = 1.0 / smooth_tau
    exp_scale = inv_tau * math.log2(math.e)
    chunk = min(lane_chunk, group)
    wide = 2 * lanes_q

    me = lax.axis_index("pages")
    y = lax.axis_index("queries")
    core = lax.rem(me, 2)
    chip = lax.div(me, 2)
    z = lax.rem(chip, NZ)
    x = lax.div(chip, NZ)

    def device(xx, yy, zz, cc):
        return ((xx * NZ + zz) * 2 + cc, yy)

    def along(pos, step, count):
        return lax.rem(pos + step, count)

    partner = device(x, y, z, 1 - core)
    z_steps = ring_offsets(NZ)[1:]
    y_steps = ring_offsets(NY)
    xy_steps = [(dx, dy) for dy in y_steps for dx in ring_offsets(NX) if (dx, dy) != (0, 0)]

    def remote(src, dst, ssem, rsem, target):
        return pltpu.make_async_remote_copy(
            src_ref=src, dst_ref=dst, send_sem=ssem, recv_sem=rsem,
            device_id=target, device_id_type=MESH,
        )

    barrier = pltpu.get_barrier_semaphore()

    def greet(target):
        pl.semaphore_signal(barrier, inc=1, device_id=target, device_id_type=MESH)

    for d in reversed(z_steps):
        greet(device(x, y, along(z, d, NZ), core))
    for dx, dy in xy_steps:
        greet(device(along(x, dx, NX), along(y, dy, NY), z, core))
    greet(partner)

    my_tokens = tok_ref.at[0, pl.ds(pl.multiple_of(y * part, part), part), :]
    own_pages = pl.ds(core * 2, 2)
    own_counts = pltpu.make_async_copy(cnt_ref, counts, local_sem.at[2])
    own_counts.start()
    own_pos = pltpu.make_async_copy(pos_ref, pos_row, local_sem.at[3])
    own_pos.start()
    own_tokens = pltpu.make_async_copy(my_tokens, zbuf.at[z], local_sem.at[0])
    own_tokens.start()
    own_patches = pltpu.make_async_copy(pat_ref, pbuf.at[own_pages], local_sem.at[1])
    own_patches.start()
    own_counts.wait()
    for i in range(2):
        cbuf[core, pl.ds(i, 1), :] = jnp.full((1, cbuf.shape[2]), counts[i], jnp.int32).astype(f32)

    pl.semaphore_wait(barrier, len(z_steps) + len(xy_steps) + 1)

    z_copies = []
    for d in reversed(z_steps):
        copy = remote(
            my_tokens, zbuf.at[z], z_send.at[d], z_recv.at[d], device(x, y, along(z, d, NZ), core)
        )
        copy.start()
        z_copies.append(copy)
    swap_patches = remote(
        pat_ref, pbuf.at[own_pages], core_send.at[0], core_recv.at[0], partner
    )
    swap_patches.start()
    swap_counts = remote(cbuf.at[core], cbuf.at[core], core_send.at[1], core_recv.at[1], partner)
    swap_counts.start()

    own_patches.wait()
    swap_counts.wait_recv()
    swap_patches.wait_recv()
    depth = pbuf.shape[2]
    slot = y * slab + lax.broadcasted_iota(jnp.int32, (slab, depth), 0)
    first_lane = lax.broadcasted_iota(jnp.int32, (slab, depth), 1) == 0
    for p in range(4):
        count = cbuf[p // 2, pl.ds(p % 2, 1), :].astype(jnp.int32)
        dead = jnp.logical_and(slot >= count, first_lane)
        bias[p] = jnp.where(dead, neg_large, 0.0).astype(bf16)
        ptran[:, p * slab : (p + 1) * slab] = pbuf[p].astype(f32).T.astype(bf16)
    select = (
        lax.broadcasted_iota(jnp.int32, (2 * lanes_q, wide), 0)
        == 2 * lax.rem(lax.broadcasted_iota(jnp.int32, (2 * lanes_q, wide), 1), lanes_q) + core
    )
    own_pos.wait()
    positive = jnp.dot(
        jnp.broadcast_to(pos_row[...].astype(f32), (8, 2 * lanes_q)).astype(bf16),
        select.astype(bf16), preferred_element_type=f32,
    )[0:1]
    log_count = smooth_tau * jnp.log(
        jnp.concatenate([cbuf[0, 0:2, 0:wide], cbuf[1, 0:2, 0:wide]], axis=0)
    )

    own_tokens.wait()
    for copy in z_copies:
        copy.wait_recv()
    zflat[...] = zbuf[...].astype(f32).reshape(zflat.shape)
    for t in range(part):
        gbuf[y * part + t, x] = zflat[pl.ds(t, NZ, stride=part), :].astype(bf16)

    pieces = group // chunk
    rows_t = chunk // lanes_q
    g_copies = {}
    for dx, dy in xy_steps:
        count = pieces if dy == y_steps[-1] else 1
        for h in range(count):
            n = (h * NY + dy) * NX + dx
            mine = gbuf.at[pl.ds(y * part + h * (part // count), part // count), x]
            g_copies[dx, dy, h] = remote(
                mine, mine, g_send.at[n], g_recv.at[n],
                device(along(x, dx, NX), along(y, dy, NY), z, core),
            )
    for (dx, dy, h), copy in sorted(
        g_copies.items(), key=lambda item: (y_steps.index(item[0][1]), item[0][2])
    ):
        copy.start()

    ones = jnp.where(lax.broadcasted_iota(jnp.int32, (chunk, depth), 1) == 0, 1.0, 0.0).astype(bf16)
    l_copies = []
    for k, back in enumerate(y_steps):
        def arrive(h):
            for dx in range(NX):
                if (dx, back, h) in g_copies:
                    g_copies[dx, back, h].wait_recv()

        arrive(0)
        gy = along(y, NY - back, NY)

        def scores(block):
            p, piece = block % 4, block // 4
            tokens = gbuf[pl.ds(gy * part + piece * rows_t, rows_t)].reshape(chunk, depth)
            similar = lax.dot_general(
                jnp.concatenate([pbuf[p], bias[p]], axis=1),
                jnp.concatenate([tokens, ones], axis=1),
                (((1,), (1,)), ((), ())), preferred_element_type=f32,
            )
            held[block % 2][...] = similar
            return jnp.max(similar, axis=0, keepdims=True)

        def exponents(block, top):
            p, piece = block % 4, block // 4
            lanes = slice(piece * chunk, (piece + 1) * chunk)
            terms = jnp.exp2((held[block % 2][...] - top) * exp_scale)
            ebuf[gy, p, :, lanes] = terms
            total = jnp.sum(terms, axis=0, keepdims=True)
            mbuf[gy, p : p + 1, lanes] = top
            lbuf[y, gy, p : p + 1, lanes] = top + smooth_tau * jnp.log(total)

        blocks = 4 * (group // chunk)
        top = scores(0)
        for block in range(blocks):
            after = block + 1
            late = after < blocks and after % 4 == 0 and back == y_steps[-1]
            if late:
                exponents(block, top)
                arrive(after // 4)
            following = scores(after) if after < blocks else None
            if not late:
                exponents(block, top)
            top = following
        for n, dy in enumerate(y_steps[1:]):
            copy = remote(
                lbuf.at[y, gy], lbuf.at[y, gy], l_send.at[k, n], l_recv.at[k, n],
                device(x, along(y, dy, NY), z, core),
            )
            copy.start()
            l_copies.append(copy)

    for copy in l_copies:
        copy.wait_recv()
    sums = jnp.zeros((4, wide), f32)
    for g in range(NY):
        lse = merge_lse(lbuf[:, g], inv_tau)
        erbuf[g] = jnp.exp((mbuf[g] - lse) * inv_tau)
        for i in range(group // wide):
            sums = sums + lse[:, i * wide : (i + 1) * wide]
    sums = sums + pltpu.roll(sums, lanes_q, 1)
    logits = (sums - query_len * log_count) / page_temp
    page_id = (chip * 4 + lax.broadcasted_iota(jnp.int32, (4, wide), 0)).astype(f32)
    is_positive = page_id == positive

    low = lax.broadcasted_iota(jnp.int32, (1, wide), 1) < lanes_q
    here = x * NZ + z
    softs[here] = jnp.where(
        low, merge_lse(logits[:, None, :], 1.0),
        jnp.sum(jnp.where(is_positive, logits, 0.0), axis=0, keepdims=True),
    )
    s_copies = []
    for d in reversed(ring_offsets(NZ)):
        for dx in reversed(ring_offsets(NX)):
            if (dx, d) == (0, 0):
                continue
            copy = remote(
                softs.at[here], softs.at[here], s_send.at[dx, d], s_recv.at[dx, d],
                device(along(x, dx, NX), y, along(z, d, NZ), core),
            )
            copy.start()
            s_copies.append(copy)
    for copy in s_copies:
        copy.wait_recv()
    everyone = softs[...]
    all_lse = merge_lse(everyone, 1.0)
    all_lse = jnp.where(low, all_lse, pltpu.roll(all_lse, lanes_q, 1))
    all_pos = jnp.sum(everyone, axis=0)
    lossbuf[core] = all_lse - pltpu.roll(all_pos, lanes_q, 1)
    swap_loss = remote(lossbuf.at[core], lossbuf.at[core], core_send.at[2], core_recv.at[2], partner)
    swap_loss.start()
    weights = (jnp.exp(logits - all_lse) - is_positive.astype(f32)) / page_temp
    wide_weights = jnp.concatenate([weights] * (group // wide), axis=1)
    for g in range(NY):
        rbuf[g] = erbuf[g] * wide_weights

    r_copies = []
    for back in reversed(y_steps):
        gy = along(y, NY - back, NY)

        for piece in range(pieces):
            lanes = slice(piece * chunk, (piece + 1) * chunk)

            def backward(p, carry):
                coef[gy, p, :, lanes] = (
                    ebuf[gy, p, :, lanes] * rbuf[gy, pl.ds(p, 1), lanes]
                ).astype(bf16)
                return carry

            lax.fori_loop(0, 4, backward, 0)
            across = jnp.dot(
                ptran[...], coef[gy, :, :, lanes].reshape(4 * slab, chunk),
                preferred_element_type=f32,
            )
            rows = across.T.reshape(rows_t, NX, NZ, depth)
            sendbuf[pl.ds(gy * part + piece * rows_t, rows_t)] = rows.astype(bf16)
            if back == 0:
                ownbuf[pl.ds(piece * rows_t, rows_t)] = rows
            dy = (NY - back) % NY
            for dx in reversed(ring_offsets(NX)):
                if (dx, dy) == (0, 0):
                    continue
                n = (piece * NY + dy) * NX + dx
                xx = along(x, dx, NX)
                copy = remote(
                    sendbuf.at[pl.ds(gy * part + piece * rows_t, rows_t), xx],
                    recvbuf.at[x * NY + y, pl.ds(piece * rows_t, rows_t)],
                    r_send.at[n], r_recv.at[n], device(xx, gy, z, core),
                )
                copy.start()
                r_copies.append((copy, dx, dy, piece))

    def page_part(p):
        total = jnp.zeros((slab, depth), f32)
        for g in range(NY):
            tokens = gbuf[g * part : (g + 1) * part].reshape(group, depth)
            total = total + jnp.dot(coef[g, p], tokens, preferred_element_type=f32)
        return total

    def other_pages(i, carry):
        pgsend[i] = page_part(2 * (1 - core) + i)
        return carry

    lax.fori_loop(0, 2, other_pages, 0)
    swap_grads = remote(pgsend, pgrecv, core_send.at[3], core_recv.at[3], partner)
    swap_grads.start()

    total = ownbuf[:, pl.ds(x, 1)].reshape(part * NZ, depth)
    for copy, dx, dy, piece in sorted(r_copies, key=lambda item: item[3]):
        copy.wait_recv()
        if piece + 1 < pieces:
            continue
        source = along(x, NX - dx, NX) * NY + along(y, NY - dy, NY)
        total = total + recvbuf[source].astype(f32).reshape(part * NZ, depth)
    zsum[...] = total
    for zz in range(NZ):
        zsend[zz] = zsum[pl.ds(zz, part, stride=NZ), :]
    q_copies = []
    for d in reversed(z_steps):
        zz = along(z, d, NZ)
        copy = remote(
            zsend.at[zz], zrecv.at[z], q_send.at[d], q_recv.at[d], device(x, y, zz, core)
        )
        copy.start()
        q_copies.append((copy, d))

    def own_page(i, carry):
        pg_ref[i] = page_part(2 * core + i)
        return carry

    lax.fori_loop(0, 2, own_page, 0)
    swap_grads.wait_recv()
    pg_ref[...] += pgrecv[...]

    swap_loss.wait_recv()
    row = lax.broadcasted_iota(jnp.int32, (wide, 2 * lanes_q), 0)
    col = lax.broadcasted_iota(jnp.int32, (wide, 2 * lanes_q), 1)
    loss = jnp.zeros((1, 2 * lanes_q), f32)
    for c in range(2):
        spread = jnp.logical_and(col == 2 * row + c, row < lanes_q).astype(f32).astype(bf16)
        loss = loss + onehot_dot(lossbuf[c], spread)
    loss_ref[...] = loss

    total = zsend[z]
    for copy, d in q_copies:
        copy.wait_recv()
        total = total + zrecv[along(z, NZ - d, NZ)]
    qg_ref[0] = total

    for copy in z_copies + list(g_copies.values()) + l_copies + s_copies:
        copy.wait_send()
    for copy in [swap_patches, swap_counts, swap_loss, swap_grads]:
        copy.wait_send()
    for copy, *_ in r_copies + q_copies:
        copy.wait_send()


def hand_on(*refs):
    sources, targets, sem = refs[:3], refs[3:6], refs[6]
    copies = [pltpu.make_async_copy(s, t, sem.at[i]) for i, (s, t) in enumerate(zip(sources, targets))]
    for copy in copies:
        copy.start()
    for copy in copies:
        copy.wait()


def shards(sizes, query_tokens, page_patches, patch_counts, positive_page):
    NX, NY, NZ = sizes
    _, query_len, depth = query_tokens.shape
    slab = page_patches.shape[1]
    part = query_len // NY
    lanes_q = NX * NZ
    group = part * lanes_q
    wide = 2 * lanes_q
    pieces = group // min(lane_chunk, group)
    vmem = pltpu.VMEM
    dma = pltpu.SemaphoreType.DMA
    shapes = [
        jax.ShapeDtypeStruct((2, slab, depth), f32),
        jax.ShapeDtypeStruct((1, part, depth), f32),
        jax.ShapeDtypeStruct((1, 2 * lanes_q), f32),
    ]
    hbm = pl.BlockSpec(memory_space=pltpu.HBM)
    loss, query_grad, page_grad = pl.pallas_call(
        functools.partial(kernel, sizes),
        out_shape=[vmem(shape.shape, f32) for shape in shapes[::-1]],
        in_specs=[hbm] * 4,
        out_specs=[pl.BlockSpec(memory_space=pltpu.VMEM)] * 3,
        scratch_shapes=[
            pltpu.SMEM((2,), jnp.int32),
            vmem((1, 2 * lanes_q), jnp.int32),
            vmem((NZ, part, depth), bf16),
            vmem((NZ * part, depth), f32),
            vmem((query_len, NX, NZ, depth), bf16),
            vmem((4, slab, depth), bf16),
            vmem((4, slab, depth), bf16),
            vmem((depth, 4 * slab), bf16),
            vmem((2, 8, depth), f32),
            vmem((NY, 4, slab, group), f32),
            vmem((NY, 4, slab, group), bf16),
            vmem((NY, 4, group), f32),
            vmem((NY, NY, 4, group), f32),
            vmem((NY, 4, group), f32),
            vmem((NY, 4, group), f32),
            vmem((slab, min(lane_chunk, group)), f32),
            vmem((slab, min(lane_chunk, group)), f32),
            vmem((NX * NZ, 1, wide), f32),
            vmem((2, 1, wide), f32),
            vmem((query_len, NX, NZ, depth), bf16),
            vmem((part, NX, NZ, depth), f32),
            vmem((NX * NY, part, NZ, depth), bf16),
            vmem((part * NZ, depth), f32),
            vmem((NZ, part, depth), f32),
            vmem((NZ, part, depth), f32),
            vmem((2, slab, depth), f32),
            vmem((2, slab, depth), f32),
            dma((4,)),
            dma((4,)), dma((4,)),
            dma((NZ,)), dma((NZ,)),
            dma((pieces * NX * NY,)), dma((pieces * NX * NY,)),
            dma((NY, NY - 1)), dma((NY, NY - 1)),
            dma((NX, NZ)), dma((NX, NZ)),
            dma((pieces * NX * NY,)), dma((pieces * NX * NY,)),
            dma((NZ,)), dma((NZ,)),
        ],
        compiler_params=pltpu.CompilerParams(
            collective_id=0, has_side_effects=True, vmem_limit_bytes=56 * 1024 * 1024
        ),
    )(query_tokens, page_patches, patch_counts, positive_page.reshape(1, 2 * lanes_q))
    page_grad, query_grad, loss = pl.pallas_call(
        hand_on,
        out_shape=shapes,
        in_specs=[pl.BlockSpec(memory_space=pltpu.VMEM)] * 3,
        out_specs=[hbm] * 3,
        scratch_shapes=[dma((3,))],
    )(*(pltpu.with_memory_space_constraint(a, pltpu.VMEM) for a in (page_grad, query_grad, loss)))
    return (loss.reshape(2 * lanes_q), query_grad, page_grad)


def solution(mesh):
    chips = mesh.shape["pages"] // 2
    sizes = (chips // chips_z, mesh.shape["queries"], chips_z)
    in_specs = (P("pages", None, None), P("pages", "queries", None), P("pages"), P())
    out_specs = (P(), P("pages", "queries", None), P("pages", "queries", None))
    return jax.shard_map(
        functools.partial(shards, sizes),
        mesh=mesh, in_specs=in_specs, out_specs=out_specs, check_vma=False,
    )
```
